32 devices in a mesh: leaf: 32 (over z, y, x, core).
Axes of the slice: x: 2, y: 2, z: 4, core: 2. Of those that a mesh axis runs over, the one named last changes fastest.
Arguments:
- points: float32 [3, 131072], P(None, 'leaf'), may hold values from 0 to 1
- rhs: float32 [16, 131072], P(None, 'leaf'), may hold values from -6 to 6
- leaf_basis: float32 [32, 131072], P(None, 'leaf'), may hold values from -0.75 to 0.75
- transfer: float32 [32, 32, 2688], P(None, None, 'leaf'), may hold values from -0.5 to 0.5
- proxies: float32 [3, 32, 2720], P(None, None, 'leaf'), may hold values from 0 to 1
- near_list: int32 [2048, 5], P('leaf'), may hold values from -1 to 2047, as said below
- couple_list: int32 [2688, 20], P('leaf'), may hold values from -1 to 2047, as said below
- root_list: int32 [32, 32], P('leaf'), may hold values from -1 to 31, as said below
Outputs:
- product: float32 [16, 131072], P(None, 'leaf')
The draws below stay inside these ranges and needn't reach their ends.
Inputs may be any that keep to these rules, and one draw needn't show every extreme that they name: `near_list`: entry [t, j] is the leaf t + j - 2 if the block of leaves t and t + j - 2 is near, else -1; every leaf is near itself. Nearness is defined level by level: at level 0 roots t and s are near when they differ by at most a per-root reach of 1 to 2 (the larger of the two); below, two clusters are near when their parents are near and they differ by at most the larger of their reaches. Near leaf blocks, with the coupled pairs of the other two lists, cover every pair of points exactly once. `couple_list`: the row of a cluster t of level l lists in slot j the cluster s = 4 * (t // 4 - 2) + j of level l if s exists, the parents of t and s are near and t and s are not near, else -1. `root_list`: entry [t, s] is s if roots t and s are not near, else -1.
All inputs are finite; a program needn't handle non-finite values.
Results may differ from the reference program's by a relative error of at most 0.0003.
Values sent between devices are 32-bit elements; how exact they have to be, the bound alone decides.
No kernel may reach another device: no remote copies, remote signals or barrier semaphores. Data moves between devices by JAX's collectives and lax.ppermute only.
A program may use at most 128 MiB of HBM per device.

```python
import math
import jax
import jax.numpy as jnp
from jax import lax

RANK = 32
NVEC = 16
LEAF = 64
LEVELS = 3
REACH = 2
FAR_SLOTS = 20
LEAF_DEV = 64
TR_DEV = 84
PX_DEV = 85
ROOTS = 32
LEAVES = 2048
NPTS = 131072
N_LEAF = 32


def closeness(key):
    masks = []
    for level_no in range(LEVELS + 1):
        clusters = ROOTS * 4 ** level_no
        reaches = jax.random.randint(jax.random.fold_in(key, 11 + level_no), (clusters,), 1, REACH + 1)
        target = jnp.arange(clusters, dtype=jnp.int32)[:, None]
        offset = jnp.arange(-REACH, REACH + 1, dtype=jnp.int32)[None, :]
        source = target + offset
        inside = (source >= 0) & (source < clusters)
        clipped = jnp.clip(source, 0, clusters - 1)
        is_near = inside & (jnp.abs(offset) <= jnp.maximum(reaches[:, None], reaches[clipped]))
        if level_no > 0:
            parent_rows = masks[-1][target[:, 0] // 4]
            column = jnp.clip(source // 4 - target // 4 + REACH, 0, 2 * REACH)
            is_near = is_near & jnp.take_along_axis(parent_rows, column, axis=1)
        masks.append(is_near)
    return masks


def far_entries(masks, level_no):
    clusters = ROOTS * 4 ** level_no
    target = jnp.arange(clusters, dtype=jnp.int32)[:, None]
    slot = jnp.arange(FAR_SLOTS, dtype=jnp.int32)[None, :]
    parent = target // 4
    source = 4 * (parent - REACH) + slot
    inside = (source >= 0) & (source < clusters)
    parent_close = jnp.take_along_axis(masks[level_no - 1][parent[:, 0]], jnp.broadcast_to(slot // 4, (clusters, FAR_SLOTS)), axis=1)
    gap = source - target
    own_close = jnp.take_along_axis(masks[level_no], jnp.clip(gap + REACH, 0, 2 * REACH), axis=1)
    is_close = (jnp.abs(gap) <= REACH) & own_close
    is_far = inside & parent_close & jnp.logical_not(is_close)
    return jnp.where(is_far, source, -1).astype(jnp.int32)


def draw_near_list(key, part):
    masks = closeness(jax.random.fold_in(key, 5))
    target = jnp.arange(ROOTS * LEAF_DEV, dtype=jnp.int32)[:, None]
    offset = jnp.arange(-REACH, REACH + 1, dtype=jnp.int32)[None, :]
    return jnp.where(masks[LEVELS], target + offset, -1).astype(jnp.int32)


def draw_couple_list(key, part):
    masks = closeness(jax.random.fold_in(key, 5))
    blocks = []
    for level_no in range(1, LEVELS + 1):
        blocks.append(far_entries(masks, level_no).reshape(ROOTS, 4 ** level_no, FAR_SLOTS))
    return jnp.concatenate(blocks, axis=1).reshape(ROOTS * TR_DEV, FAR_SLOTS)


def draw_root_list(key, part):
    masks = closeness(jax.random.fold_in(key, 5))
    target = jnp.arange(ROOTS, dtype=jnp.int32)[:, None]
    source = jnp.arange(ROOTS, dtype=jnp.int32)[None, :]
    gap = source - target
    own_close = jnp.take_along_axis(masks[0], jnp.clip(gap + REACH, 0, 2 * REACH), axis=1)
    is_close = (jnp.abs(gap) <= REACH) & own_close
    return jnp.where(is_close, -1, jnp.broadcast_to(source, (ROOTS, ROOTS))).astype(jnp.int32)


def block_scale(rng, shape, shards, low, top_value):
    def one(position, blocks):
        draws = jax.random.uniform(jax.random.fold_in(jax.random.fold_in(rng, 6), position), (blocks,), jnp.float32, low / len(shards), top_value / len(shards))
        return jnp.repeat(jnp.exp(draws), shape[position] // blocks).reshape((-1,) + (1,) * (len(shape) - position - 1))

    factor_of = one(*shards[0])
    for cut in shards[1:]:
        factor_of = factor_of * one(*cut)
    return factor_of


def scatter_about(own_key, shape, width, bound, cuts=(), kind=jnp.bfloat16):
    values = width * jax.random.normal(own_key, shape, jnp.float32)
    if cuts:
        values = values * block_scale(own_key, shape, cuts, -0.22, 0.18)
    return jnp.clip(values, -bound, bound).astype(kind)


def setup_inputs(seed: int = 0) -> dict:
    streams_of = jax.random.split(jax.random.key(seed), 9)
    return {
        "points": jnp.clip(1.0 * jax.random.uniform(streams_of[0], (3, NPTS), jnp.float32) ** block_scale(streams_of[0], (3, NPTS), ((1, 32),), -0.2, 0.2), 0.0, 1.0),
        "rhs": scatter_about(streams_of[1], (NVEC, NPTS), 1.0, 6.0, ((1, 32),), jnp.float32),
        "leaf_basis": scatter_about(streams_of[2], (RANK, NPTS), LEAF ** -0.5, 0.75, ((1, 32),), jnp.float32),
        "transfer": scatter_about(streams_of[3], (RANK, RANK, TR_DEV * N_LEAF), (4 * RANK) ** -0.5, 0.5, ((2, 32),), jnp.float32),
        "proxies": jnp.clip(1.0 * jax.random.uniform(streams_of[4], (3, RANK, PX_DEV * N_LEAF), jnp.float32) ** block_scale(streams_of[4], (3, RANK, PX_DEV * N_LEAF), ((2, 32),), -0.2, 0.2), 0.0, 1.0),
        "near_list": draw_near_list(jax.random.fold_in(streams_of[8], 71), 0),
        "couple_list": draw_couple_list(jax.random.fold_in(streams_of[8], 71), 0),
        "root_list": draw_root_list(jax.random.fold_in(streams_of[8], 71), 0),
    }


kernel_band = 0.1
highest = lax.Precision.HIGHEST


def kernel_sq(left_pts, right_pts):
    length = (left_pts[0] - right_pts[0]) ** 2 + (left_pts[1] - right_pts[1]) ** 2 + (left_pts[2] - right_pts[2]) ** 2
    return jnp.exp(-length / kernel_band)


def by_blocks(method, inputs, length, stride, out_shape):
    stride = math.gcd(length, stride)

    def advance(step_no, accumulated):
        begin_at = step_no * stride
        pieces = [lax.dynamic_slice_in_dim(operand, begin_at, stride, operand.ndim - 1) for operand in inputs]
        return lax.dynamic_update_slice_in_dim(accumulated, method(*pieces), begin_at, accumulated.ndim - 1)

    return lax.fori_loop(0, length // stride, advance, jnp.zeros(out_shape, jnp.float32))


def couple(target_prox, lookup, source_prox, listed):
    usable = listed.T >= 0
    clipped = jnp.where(usable, listed.T, 0)

    def one_block(target_blk, clipped_blk, usable_blk):
        coeff_blk = jnp.take(lookup, clipped_blk, axis=2)
        prox_blk = jnp.take(source_prox, clipped_blk, axis=2)
        kernel = kernel_sq(target_blk[:, :, None, None, :], prox_blk[:, None, :, :, :]) * usable_blk.astype(coeff_blk.dtype)
        return jnp.einsum('absn,bksn->akn', kernel, coeff_blk, precision=highest)

    extent = listed.shape[0]
    return by_blocks(one_block, [target_prox, clipped, usable], extent, 128, (lookup.shape[0], lookup.shape[1], extent))


def near_field(targets, lookup, listed, vectors):
    usable = listed.T >= 0
    clipped = jnp.where(usable, listed.T, 0)

    def one_block(target_blk, clipped_blk, usable_blk):
        source = jnp.take(lookup, clipped_blk, axis=2)
        kernel = kernel_sq(target_blk[:, :, None, None, :], source[vectors:, None, :, :, :]) * usable_blk.astype(source.dtype)
        return jnp.einsum('ijsn,kjsn->kin', kernel, source[:vectors], precision=highest)

    extent = listed.shape[0]
    return by_blocks(one_block, [targets, clipped, usable], extent, 128, (vectors, targets.shape[1], extent))


def reference(points, rhs, leaf_basis, transfer, proxies, near_list, couple_list, root_list):
    basis_grid = leaf_basis.reshape(RANK, LEAVES, LEAF)
    coeffs = [None] * (LEVELS + 1)
    coeffs[LEVELS] = jnp.einsum('rnp,knp->rkn', basis_grid, rhs.reshape(NVEC, LEAVES, LEAF), precision=highest)
    proxy_grid = proxies.reshape(3, RANK, ROOTS, PX_DEV)
    transfer_grid = transfer.reshape(RANK, RANK, ROOTS, TR_DEV)
    list_grid = couple_list.reshape(ROOTS, TR_DEV, FAR_SLOTS)
    level_prox = []
    mappings = [None]
    entries = [None]
    for level_no in range(LEVELS + 1):
        extent = 4 ** level_no
        begin_at = (extent - 1) // 3
        level_prox.append(proxy_grid[:, :, :, begin_at:begin_at + extent].reshape(3, RANK, ROOTS * extent))
        if level_no > 0:
            mappings.append(transfer_grid[:, :, :, begin_at - 1:begin_at - 1 + extent].reshape(RANK, RANK, ROOTS * extent))
            entries.append(list_grid[:, begin_at - 1:begin_at - 1 + extent].reshape(ROOTS * extent, FAR_SLOTS))
    for level_no in range(LEVELS, 0, -1):
        merged = jnp.einsum('abn,akn->bkn', mappings[level_no], coeffs[level_no], precision=highest)
        coeffs[level_no - 1] = merged.reshape(RANK, NVEC, -1, 4).sum(axis=3)
    coupled = []
    for level_no in range(LEVELS + 1):
        listed = root_list if level_no == 0 else entries[level_no]
        coupled.append(couple(level_prox[level_no], coeffs[level_no], level_prox[level_no], listed))
    downward = coupled[0]
    for level_no in range(1, LEVELS + 1):
        downward = coupled[level_no] + jnp.einsum('abn,bkn->akn', mappings[level_no], jnp.repeat(downward, 4, axis=2), precision=highest)
    lookup_pts = jnp.concatenate([rhs, points], axis=0).reshape(NVEC + 3, LEAVES, LEAF).transpose(0, 2, 1)
    targets = points.reshape(3, LEAVES, LEAF).transpose(0, 2, 1)
    near_part = near_field(targets, lookup_pts, near_list, NVEC)
    far_part = jnp.einsum('rnp,rkn->knp', basis_grid, downward, precision=highest)
    return (near_part.transpose(0, 2, 1) + far_part).reshape(NVEC, NPTS)
```

```python
import math

import jax
import jax.numpy as jnp
from jax import lax
from jax.experimental import pallas as pl
from jax.experimental.pallas import tpu as pltpu
from jax.sharding import PartitionSpec as P

LEVELS = 3
REACH = 2
FAN = 4
LANES = 128
ROWS = 24
FEATS = 32
SCALE = 10.0 * math.log2(math.e)
F32 = jnp.float32
BF16 = jnp.bfloat16

NN = (((1,), (0,)), ((), ()))
NT = (((1,), (1,)), ((), ()))
TN = (((0,), (0,)), ((), ()))


def dot(lhs, rhs, dims=NN):
    return lax.dot_general(lhs, rhs, dims, preferred_element_type=F32)


def split2(value):
    high = value.astype(BF16)
    low = (value - high.astype(F32)).astype(BF16)
    return high, low


def split3(value):
    high = value.astype(BF16).astype(F32)
    rest = value - high
    mid = rest.astype(BF16).astype(F32)
    return high, mid, rest - mid


def stack2(value):
    high, low = split2(value)
    return high, jnp.concatenate([high, low], axis=0)


def dot2(lhs, rhs, dims=NN):
    high, both = stack2(lhs)
    rhs_high, rhs_low = split2(rhs)
    rows = lhs.shape[0]
    wide = dot(both, rhs_high, dims)
    return wide[:rows] + wide[rows:] + dot(high, rhs_low, dims)


def iota(shape, axis):
    return lax.broadcasted_iota(jnp.int32, shape, axis)


def spread(clusters, width, begin, size):
    shape = (clusters, width)
    return (iota(shape, 0) == begin + iota(shape, 1) // size).astype(BF16)


def block_rows(basis, offset, leaf):
    part = basis[:, pl.ds(offset, FAN * leaf)]
    rank = part.shape[0]
    tiled = jnp.concatenate([part] * FAN, axis=0)
    keep = iota(tiled.shape, 0) // rank == iota(tiled.shape, 1) // leaf
    return jnp.where(keep, tiled, 0.0)


def upward_kernel(
    rhs, points, basis, transfer, prox, c3, c2, c1, tile0, right, left, *, leaf, rank, starts
):
    vectors = rhs.shape[0]
    span = FAN * leaf
    group = FAN * rank
    outs = {1: c1, 2: c2, 3: c3}
    for g in range(rhs.shape[1] // span):
        big = block_rows(basis, g * span, leaf)
        c3[:vectors, g * group : (g + 1) * group] = dot2(
            rhs[:, g * span : (g + 1) * span], big, NT
        )
    keep = None
    for level in range(LEVELS, 0, -1):
        source = outs[level]
        count = FAN ** (level - 1)
        base = (starts[level] - 1) * rank
        per = min(FAN, count)
        for h in range(count // per):
            width = per * group
            begin = h * width
            weights = transfer[base + begin : base + begin + width, :]
            keep = iota(weights.shape, 0) // group == iota(weights.shape, 1) // rank
            weights = jnp.where(keep, weights, 0.0)
            merged = dot2(source[:vectors, begin : begin + width], weights)
            if level > 1:
                outs[level - 1][:vectors, h * group : (h + 1) * group] = merged
            else:
                root = merged
    coords = prox.shape[0] // rank
    parts = jnp.concatenate(split3(prox[...]), axis=0).astype(BF16)
    clusters = prox.shape[1]
    for level in range(LEVELS + 1):
        total = max(FAN**level * rank, LANES)
        step = min(total, 512)
        for begin in range(0, total, step):
            cols = spread(clusters, step, starts[level] + begin // rank, rank)
            if level == 0:
                cols = jnp.where(iota(cols.shape, 1) < rank, cols, jnp.zeros_like(cols))
            rows = dot(parts, cols)
            n = coords * rank
            rows = rows[:n] + rows[n : 2 * n] + rows[2 * n :]
            rows = jnp.where(iota(rows.shape, 0) % rank == iota(rows.shape, 1) % rank, rows, 0.0)
            for c in range(coords):
                line = jnp.sum(rows[c * rank : (c + 1) * rank], axis=0, keepdims=True)
                if level == 0:
                    tile0[c : c + 1, :] = line
                else:
                    outs[level][vectors + c : vectors + c + 1, begin : begin + step] = line
    lane = iota((8, LANES), 1)
    for c in range(coords, 8):
        tile0[c : c + 1, :] = jnp.zeros((1, LANES), F32)
    prox_tile = pltpu.roll(tile0[...], 2 * rank, 1)
    lower = jnp.where(lane < rank, root[:8], 0.0)
    upper = pltpu.roll(jnp.where(lane < rank, root[8:16], 0.0), rank, 1)
    tile0[...] = lower + upper + prox_tile
    for level in (1, 2, 3):
        pad = outs[level]
        pad[vectors + coords :, :] = jnp.zeros(
            (ROWS - vectors - coords, pad.shape[1]), F32
        )
    rim = 2 * group
    for send, tail in ((right, True), (left, False)):
        at = 0
        for ref, width in ((c3, rim), (c2, rim), (c1, group)):
            begin = ref.shape[1] - width if tail else 0
            send[:, at : at + width] = ref[:, begin : begin + width]
            at += width
        begin = points.shape[1] - REACH * leaf if tail else 0
        send[:vectors, at:] = rhs[:, begin : begin + REACH * leaf]
        send[vectors : vectors + coords, at:] = points[:, begin : begin + REACH * leaf]
        send[vectors + coords :, at:] = jnp.zeros((ROWS - vectors - coords, REACH * leaf), F32)


def features(position, feats):
    centred = position - 0.5
    high, mid, low = split3(centred)
    wide = centred * (2.0 * SCALE)
    w_high, w_mid, w_low = split3(wide)
    norm = -SCALE * jnp.sum(centred * centred, axis=0, keepdims=True)
    n_parts = split3(norm)
    n = position.shape[1]
    for row, part in enumerate((high, high, high, mid, mid, low)):
        feats[0, 3 * row : 3 * row + 3, :n] = part
    for row, part in enumerate((w_high, w_mid, w_low, w_high, w_mid, w_high)):
        feats[1, 3 * row : 3 * row + 3, :n] = part
    one = jnp.ones((3, n), F32)
    feats[0, 21:24, :n] = one
    feats[1, 18:21, :n] = one
    for row, part in enumerate(n_parts):
        feats[0, 18 + row : 19 + row, :n] = part
        feats[1, 21 + row : 22 + row, :n] = part
    zero = jnp.zeros((FEATS - 24, n), F32)
    feats[0, 24:, :n] = zero
    feats[1, 24:, :n] = zero


def to_rows(feats, rows, begin, n):
    for at in range(0, n, LANES):
        rows[begin + at : begin + at + LANES, :] = jnp.transpose(
            feats[0, :, at : at + LANES]
        ).astype(BF16)


def apply_kernel(kernel, both, vectors):
    high, low = split2(kernel)
    wide = dot(both, high)
    return wide[:vectors] + wide[vectors:] + dot(both[:vectors], low)


def final_kernel(
    device, rhs, points, basis, transfer, near, couple, roots, c3, c2, c1, tile0, gathered,
    from_left, from_right, second_left, second_right, out,
    feats, src, tgt, coef, near_mask, far_mask, field, field2,
    *, leaf, rank, starts, xor,
):
    vectors = rhs.shape[0]
    coords = points.shape[0]
    group = FAN * rank
    rim = 2 * group
    n_points = rhs.shape[1]
    n_leaves = n_points // leaf
    top = vectors + coords

    listed = (near[...] >= 0).astype(F32).astype(BF16)
    near_mask[...] = jnp.zeros(near_mask.shape, F32)
    for at in range(0, n_points, 1024):
        cols = spread(n_leaves, 1024, at // leaf, leaf)
        rows = dot(listed, cols, TN)
        odd = (iota(rows.shape, 1) // leaf) % 2 == 1
        slots = rows.shape[0]
        near_mask[0:slots, at : at + 1024] = jnp.where(odd, 0.0, rows)
        near_mask[1 : slots + 1, at : at + 1024] += jnp.where(odd, rows, 0.0)
    listed = (couple[...] >= 0).astype(F32).astype(BF16)
    n_far = couple.shape[0] * rank
    for at in range(0, n_far, 384):
        cols = spread(couple.shape[0], 384, at // rank, rank)
        far_mask[0 : couple.shape[1], at : at + 384] = dot(listed, cols, TN)

    halo = REACH * leaf
    last = from_left.shape[1] - halo
    for begin, ref, at, n in (
        (0, from_left, last, halo),
        (halo + n_points, from_right, last, halo),
    ):
        features(ref[vectors:top, at : at + n], feats)
        to_rows(feats, src, begin, n)
        coef[:, begin : begin + n] = stack2(ref[:vectors, at : at + n])[1]
    features(points[...], feats)
    to_rows(feats, src, halo, n_points)
    tgt[:, :n_points] = feats[1, :, :n_points].astype(BF16)
    coef[:, halo : halo + n_points] = stack2(rhs[...])[1]

    def near_group(g, carry):
        begin = pl.multiple_of(g * halo, LANES)
        kernel = jnp.exp2(dot(src[pl.ds(begin, 3 * halo), :], tgt[:, pl.ds(begin, halo)]))
        mask = near_mask[:, pl.ds(begin, halo)]
        kernel = jnp.concatenate(
            [kernel[leaf * s : leaf * (s + 1)] * mask[s : s + 1] for s in range(6)], axis=0
        )
        out[:, pl.ds(begin, halo)] = apply_kernel(
            kernel, coef[:, pl.ds(begin, 3 * halo)], vectors
        )
        return carry

    lax.fori_loop(0, n_points // halo, near_group, 0, unroll=4)

    n_roots = roots.shape[1]
    n_all = n_roots * rank
    lane = iota((8, LANES), 1) // rank
    for at in range(0, n_roots, FAN):
        low = jnp.zeros((8, LANES), F32)
        up = low
        place = low
        for j in range(FAN):
            tile = gathered[at + j]
            here = lane == j
            low = jnp.where(here, pltpu.roll(tile, j * rank, 1) if j else tile, low)
            up = jnp.where(here, pltpu.roll(tile, ((j - 1) % FAN) * rank, 1) if j != 1 else tile, up)
            place = jnp.where(
                here, pltpu.roll(tile, ((j - 2) % FAN) * rank, 1) if j != 2 else tile, place
            )
        lanes = slice(at * rank, at * rank + LANES)
        field[0:8, lanes] = low
        field[8:16, lanes] = up
        field[16:24, lanes] = place
    listed = (jnp.broadcast_to(roots[...], (8, n_roots)) >= 0).astype(F32).astype(BF16)
    me = device[0]
    for at in range(0, n_all, 1024):
        shape = (n_roots, 1024)
        source = at // rank + iota(shape, 1) // rank
        if xor:
            source = jnp.bitwise_xor(source, me)
        usable = dot(listed, (iota(shape, 0) == source).astype(BF16))
        coef[:, at : at + 1024] = stack2(field[:vectors, at : at + 1024] * usable[0:1])[1]
        features(field[vectors:top, at : at + 1024], feats)
        to_rows(feats, src, at, 1024)
    features(pltpu.roll(tile0[...], LANES - 2 * rank, 1)[:coords], feats)
    tgt[:, :LANES] = feats[1, :, :LANES].astype(BF16)
    down = jnp.zeros((vectors, LANES), F32)
    for at in range(0, n_all, 512):
        kernel = jnp.exp2(dot(src[at : at + 512, :], tgt[:, :LANES]))
        down = down + apply_kernel(kernel, coef[:, at : at + 512], vectors)
    field[:vectors, :LANES] = down

    parent = field
    child = field2
    for level in range(1, LEVELS + 1):
        own = {1: c1, 2: c2, 3: c3}[level]
        width = own.shape[1]
        if level == 1:
            at = 2 * rim
            pieces = (
                (0, second_left, 0, group),
                (group, from_left, at, group),
                (2 * group, own, 0, group),
                (3 * group, from_right, at, group),
                (4 * group, second_right, 0, group),
            )
        else:
            at = 0 if level == 3 else rim
            pieces = (
                (0, from_left, at, rim),
                (rim, own, 0, width),
                (rim + width, from_right, at, rim),
            )
        for begin, ref, at, n in pieces:
            features(ref[vectors:top, at : at + n], feats)
            to_rows(feats, src, begin, n)
            if ref is own:
                tgt[:, :n] = feats[1, :, :n].astype(BF16)
            coef[:, begin : begin + n] = stack2(ref[:vectors, at : at + n])[1]
        base = (starts[level] - 1) * rank

        def far_group(q, carry, base=base, parent=parent, child=child):
            begin = q * group
            if not isinstance(q, int):
                begin = pl.multiple_of(begin, LANES)
            kernel = jnp.exp2(dot(src[pl.ds(begin, 5 * group), :], tgt[:, pl.ds(begin, group)]))
            mask = far_mask[:, pl.ds(base + begin, group)]
            kernel = jnp.concatenate(
                [kernel[rank * s : rank * (s + 1)] * mask[s : s + 1] for s in range(5 * FAN)],
                axis=0,
            )
            total = apply_kernel(kernel, coef[:, pl.ds(begin, 5 * group)], vectors)
            above = parent[:vectors, pl.ds((q // FAN) * group, group)]
            above = jnp.where(iota(above.shape, 1) // rank == q % FAN, above, 0.0)
            total = total + dot2(above, transfer[pl.ds(base + begin, group), :], NT)
            child[:vectors, pl.ds(begin, group)] = total
            return carry

        if width == group:
            far_group(0, 0)
        else:
            lax.fori_loop(0, width // group, far_group, 0, unroll=2)
        parent, child = child, parent

    span = FAN * leaf
    for g in range(n_points // span):
        big = block_rows(basis, g * span, leaf)
        out[:, g * span : (g + 1) * span] += dot2(parent[:vectors, g * group : (g + 1) * group], big)


def line(count, shift):
    return [(i, i + shift) for i in range(count) if 0 <= i + shift < count]


def body(points, rhs, leaf_basis, transfer, proxies, near_list, couple_list, root_list):
    count = lax.axis_size("leaf")
    device = lax.axis_index("leaf")
    rank = leaf_basis.shape[0]
    vectors, n_points = rhs.shape
    leaf = n_points // near_list.shape[0]
    group = FAN * rank
    starts = [(FAN**level - 1) // (FAN - 1) for level in range(LEVELS + 1)]
    n_transfer = transfer.shape[2]
    table = jnp.transpose(transfer, (2, 0, 1)).reshape(n_transfer * rank, rank)
    table = jnp.tile(table, (1, LANES // rank))
    flat_prox = proxies.reshape(proxies.shape[0] * rank, proxies.shape[2])

    vmem = pl.BlockSpec(memory_space=pltpu.VMEM)
    smem = pl.BlockSpec(memory_space=pltpu.SMEM)
    rim = 2 * group
    send = 2 * rim + group + REACH * leaf

    def shape(*dims):
        return jax.ShapeDtypeStruct(dims, F32)

    c3, c2, c1, tile0, right, left = pl.pallas_call(
        lambda *refs: upward_kernel(*refs, leaf=leaf, rank=rank, starts=starts),
        out_shape=(
            shape(ROWS, FAN**3 * rank),
            shape(ROWS, FAN**2 * rank),
            shape(ROWS, FAN * rank),
            shape(8, LANES),
            shape(ROWS, send),
            shape(ROWS, send),
        ),
        in_specs=[vmem] * 5,
        out_specs=(vmem,) * 6,
        name="upward",
    )(rhs, points, leaf_basis, table, flat_prox)

    xor = count & (count - 1) == 0
    if xor:
        gathered = tile0[None]
        step = 1
        while step < count:
            other = lax.ppermute(gathered, "leaf", [(i, i ^ step) for i in range(count)])
            gathered = jnp.concatenate([gathered, other], axis=0)
            step *= 2
    else:
        gathered = lax.all_gather(tile0, "leaf", axis=0)
    from_left = lax.ppermute(right, "leaf", line(count, 1))
    from_right = lax.ppermute(left, "leaf", line(count, -1))
    second_left = lax.ppermute(c1, "leaf", line(count, 2))
    second_right = lax.ppermute(c1, "leaf", line(count, -2))

    n_ext = n_points + 2 * REACH * leaf
    n_roots = root_list.shape[1]
    n_src = max(n_ext, n_roots * rank, 1024)
    n_couple = couple_list.shape[0]
    n_field = max(FAN**3 * rank, n_roots * rank)
    return pl.pallas_call(
        lambda *refs: final_kernel(*refs, leaf=leaf, rank=rank, starts=starts, xor=xor),
        out_shape=shape(vectors, n_points),
        in_specs=[smem] + [vmem] * 16,
        out_specs=vmem,
        scratch_shapes=[
            pltpu.VMEM((2, FEATS, n_src), F32),
            pltpu.VMEM((n_src, FEATS), BF16),
            pltpu.VMEM((FEATS, n_points), BF16),
            pltpu.VMEM((2 * vectors, n_src), BF16),
            pltpu.VMEM((8, n_points), F32),
            pltpu.VMEM((ROWS, n_couple * rank), F32),
            pltpu.VMEM((ROWS, n_field), F32),
            pltpu.VMEM((ROWS, n_field), F32),
        ],
        name="final",
    )(
        device.astype(jnp.int32)[None], rhs, points, leaf_basis, table, near_list, couple_list,
        root_list, c3, c2, c1, tile0, gathered, from_left, from_right, second_left, second_right,
    )


def solution(mesh):
    in_specs = (
        P(None, "leaf"),
        P(None, "leaf"),
        P(None, "leaf"),
        P(None, None, "leaf"),
        P(None, None, "leaf"),
        P("leaf", None),
        P("leaf", None),
        P("leaf", None),
    )
    out_specs = P(None, "leaf")
    return jax.shard_map(body, mesh=mesh, in_specs=in_specs, out_specs=out_specs, check_vma=False)
```

```python
import math

import jax
import jax.numpy as jnp
from jax import lax
from jax.experimental import pallas as pl
from jax.experimental.pallas import tpu as pltpu
from jax.sharding import PartitionSpec as P

LEVELS = 3
REACH = 2
FAN = 4
LANES = 128
ROWS = 24
FEATS = 32
SCALE = 10.0 * math.log2(math.e)
F32 = jnp.float32
BF16 = jnp.bfloat16

NN = (((1,), (0,)), ((), ()))
NT = (((1,), (1,)), ((), ()))


def dot(lhs, rhs, dims=NN):
    return lax.dot_general(lhs, rhs, dims, preferred_element_type=F32)


def iota(shape, axis):
    return lax.broadcasted_iota(jnp.int32, shape, axis)


def split2(value):
    high = value.astype(BF16)
    low = (value - high.astype(F32)).astype(BF16)
    return high, low


def split3(value):
    high = value.astype(BF16).astype(F32)
    rest = value - high
    mid = rest.astype(BF16).astype(F32)
    return high, mid, rest - mid


def stack2(value):
    high, low = split2(value)
    return jnp.concatenate([high, low], axis=0)


def dot2(both, high, low, dims=NN):
    rows = both.shape[0] // 2
    wide = dot(both, high, dims)
    return wide[:rows] + wide[rows:] + dot(both[:rows], low, dims)


def spread(clusters, width, begin, size):
    shape = (clusters, width)
    return (iota(shape, 0) == begin + iota(shape, 1) // size).astype(BF16)


def listed_mask(lists, begin, width, size):
    listed = (lists[...] >= 0).astype(F32).astype(BF16)
    return dot(listed, spread(lists.shape[1], width, begin, size))


def block_rows(basis, offset, leaf):
    part = basis[:, offset : offset + FAN * leaf]
    rank = part.shape[0]
    tiled = jnp.concatenate([part] * FAN, axis=0)
    keep = iota(tiled.shape, 0) // rank == iota(tiled.shape, 1) // leaf
    return split2(jnp.where(keep, tiled, 0.0))


def pick(groups):
    shape = (FEATS, FEATS)
    feature = iota(shape, 0)
    want = jnp.full(shape, -1, jnp.int32)
    for g, row in enumerate(groups):
        want = jnp.where(feature // 3 == g, row + feature % 3, want)
    return (iota(shape, 1) == want).astype(F32).astype(BF16)


def features(position):
    row = iota(position.shape, 0)
    centred = jnp.where(row < 3, position - 0.5, 0.0)
    norm = -SCALE * jnp.sum(centred * centred, axis=0, keepdims=True)
    tail = jnp.where((row >= 3) & (row < 6), 1.0, 0.0)
    for r, part in enumerate(split3(norm)):
        tail = jnp.where(row == r, part, tail)
    own = jnp.concatenate([*split3(centred), tail], axis=0).astype(BF16)
    other = jnp.concatenate([*split3(centred * (2.0 * SCALE)), tail], axis=0).astype(BF16)
    source = dot(pick((0, 0, 0, 8, 8, 16, 24, 27)), own)
    target = dot(pick((0, 8, 16, 0, 8, 0, 27, 24)), other)
    return source, target


def set_features(position, src, tgt, begin):
    n = position.shape[1]
    for at in range(0, n, 512):
        end = min(at + 512, n)
        source, target = features(position[:, at:end])
        if tgt is not None:
            tgt[:, begin + at : begin + end] = target.astype(BF16)
        if src is not None:
            for lane in range(0, end - at, LANES):
                to = begin + at + lane
                src[to : to + LANES, :] = jnp.transpose(source[:, lane : lane + LANES]).astype(
                    BF16
                )


def pad_rows(points):
    return jnp.concatenate([points, jnp.zeros((8 - points.shape[0], points.shape[1]), F32)], axis=0)


def fill_block(src, tgt, row, lane, n_rows, mask, size, high, low, at):
    kernel = jnp.exp2(dot(src[pl.ds(row, n_rows), :], tgt[:, pl.ds(lane, LANES)]))
    if mask is not None:
        kernel = jnp.concatenate(
            [kernel[size * s : size * (s + 1)] * mask[s : s + 1] for s in range(n_rows // size)],
            axis=0,
        )
    high[pl.ds(at, n_rows), :], low[pl.ds(at, n_rows), :] = split2(kernel)


def use_block(coef, row, n_rows, high, low, at):
    return dot2(coef[:, pl.ds(row, n_rows)], high[pl.ds(at, n_rows), :], low[pl.ds(at, n_rows), :])


def upward_kernel(
    device, rhs, points, basis, transfer, prox,
    c3, c2, c1, tile0, first, second, table_high, table_low,
    padded, moved, *, leaf, rank, starts,
):
    vectors = rhs.shape[0]
    coords = points.shape[0]
    span = FAN * leaf
    group = FAN * rank
    outs = {1: c1, 2: c2, 3: c3}

    n_clusters = transfer.shape[1]
    padded[...] = jnp.zeros(padded.shape, F32)
    padded[:, :n_clusters] = transfer[...]
    row = iota((8, LANES), 0)
    block = iota((8, LANES), 1) // rank
    for a in range(0, rank, FAN):
        flipped = jnp.transpose(padded[a * rank : (a + FAN) * rank, :])
        for t in range(0, n_clusters, 8):
            tile = flipped[t : t + 8]
            turns = [tile] + [pltpu.roll(tile, rank * s, 1) for s in range(1, FAN)]
            low = (t // FAN - 1) % FAN
            up = (t // FAN) % FAN
            in_low = (row < FAN) & (block == low)
            in_up = (row >= FAN) & (block == up)
            for j in range(FAN):
                value = jnp.where(in_up, turns[(up - j) % FAN], 0.0)
                value = jnp.where(in_low, turns[(low - j) % FAN], value)
                moved[t : t + 8, a + j, :] = value
    for t in range(0, n_clusters, FAN):
        rows = slice(t * rank, t * rank + group)
        table_high[rows, :], table_low[rows, :] = split2(
            moved[t : t + FAN].reshape(group, LANES)
        )

    for g in range(rhs.shape[1] // span):
        high, low = block_rows(basis, g * span, leaf)
        c3[:vectors, g * group : (g + 1) * group] = dot2(
            stack2(rhs[:, g * span : (g + 1) * span]), high, low, NT
        )
    for level in range(LEVELS, 0, -1):
        source = outs[level]
        count = FAN ** (level - 1)
        base = (starts[level] - 1) * rank
        per = min(FAN, count)
        width = per * group
        for h in range(count // per):
            begin = h * width
            rows = slice(base + begin, base + begin + width)
            merged = dot2(
                stack2(source[:vectors, begin : begin + width]),
                table_high[rows, :],
                table_low[rows, :],
            )
            if level > 1:
                outs[level - 1][:vectors, h * group : (h + 1) * group] = merged
            else:
                root = merged

    parts = jnp.concatenate(split3(prox[...]), axis=0).astype(BF16)
    clusters = prox.shape[1]
    n = coords * rank
    row = iota((8, LANES), 0)
    for level in range(LEVELS + 1):
        total = max(FAN**level * rank, LANES)
        step = min(total, 512)
        for begin in range(0, total, step):
            lines = dot(parts, spread(clusters, step, starts[level] + begin // rank, rank))
            lines = lines[:n] + lines[n : 2 * n] + lines[2 * n :]
            lines = jnp.where(iota(lines.shape, 0) % rank == iota(lines.shape, 1) % rank, lines, 0.0)
            rows = iota((8, step), 0)
            place = jnp.zeros((8, step), F32)
            for c in range(coords):
                line = jnp.sum(lines[c * rank : (c + 1) * rank], axis=0, keepdims=True)
                place = jnp.where(rows == c, line, place)
            if level == 0:
                root_place = place
            else:
                outs[level][vectors:, begin : begin + step] = place
    last = (FAN - 1) * rank
    tile = jnp.where(block == 0, pltpu.roll(root[:8], LANES - last, 1), 0.0)
    tile = jnp.where(block == 1, pltpu.roll(root[8:16], LANES - last + rank, 1), tile)
    tile = jnp.where(block == 2, pltpu.roll(root_place, 2 * rank, 1), tile)
    tile0[...] = tile

    rim = 2 * group
    halo = REACH * leaf

    def fill(send, tail):
        at = 0
        for ref, width in ((c3, rim), (c2, rim)):
            begin = ref.shape[1] - width if tail else 0
            send[:, at : at + width] = ref[:, begin : begin + width]
            at += width
        begin = points.shape[1] - halo if tail else 0
        send[:vectors, at : at + halo] = rhs[:, begin : begin + halo]
        send[vectors:, at : at + halo] = pad_rows(points[:, begin : begin + halo])

    @pl.when(device[0] % 2 == 0)
    def _():
        fill(first, True)
        fill(second, False)

    @pl.when(device[0] % 2 == 1)
    def _():
        fill(first, False)
        fill(second, True)

    at = 2 * rim + halo
    first[:, at : at + group] = c1[...]
    second[:, at : at + group] = c1[...]
    first[:8, at + group :] = tile
    first[8:, at + group :] = jnp.zeros((ROWS - 8, LANES), F32)


def middle_kernel(first, second, tile0, send, pair):
    width = second.shape[1]
    send[:, :width] = second[...]
    send[:, width:] = first[:, width - LANES : width]
    pair[0] = tile0[...]
    pair[1] = first[:8, width:]


def join_kernel(lower, upper, out):
    count = lower.shape[0]
    out[:count] = lower[...]
    out[count:] = upper[...]


def near_kernel(rhs, points, near, out, src, tgt, coef, mask, high, low, *, leaf, unroll):
    n_points = rhs.shape[1]
    halo = REACH * leaf
    count = n_points // halo
    set_features(pad_rows(points[...]), src, tgt, 0)
    coef[...] = stack2(rhs[...])
    for at in range(0, n_points, 1024):
        mask[:, at : at + 1024] = near_mask(near, at, 1024, leaf)

    def fill(g, carry):
        begin = pl.multiple_of(g * halo, LANES)
        fill_block(
            src, tgt, begin, pl.multiple_of(begin + halo, LANES), 3 * halo,
            mask[:, pl.ds(pl.multiple_of(begin + halo, LANES), halo)], leaf,
            high, low, pl.multiple_of(g * 3 * halo, LANES),
        )
        return carry

    def use(g, carry):
        begin = pl.multiple_of(g * halo, LANES)
        out[:, pl.ds(pl.multiple_of(begin + halo, LANES), halo)] = use_block(
            coef, begin, 3 * halo, high, low, pl.multiple_of(g * 3 * halo, LANES)
        )
        return carry

    lax.fori_loop(0, count - 2, fill, 0, unroll=unroll)
    lax.fori_loop(0, count - 2, use, 0, unroll=unroll)


def near_mask(near, begin, width, leaf):
    rows = listed_mask(near, begin // leaf, width, leaf)
    slots = rows.shape[0]
    odd = (iota((8, width), 1) // leaf) % 2 == 1
    even_rows = jnp.concatenate([rows, jnp.zeros((8 - slots, width), F32)], axis=0)
    return jnp.where(odd, pltpu.roll(even_rows, 1, 0), even_rows)


def far_kernel(
    c3, couple, basis, out, big_high, big_low, src, tgt, coef, mask, high, low,
    *, leaf, rank, base, unroll,
):
    group = FAN * rank
    vectors = out.shape[0]
    width = c3.shape[1]
    set_features(c3[vectors:, :], src, tgt, 0)
    coef[...] = stack2(c3[:vectors, :])
    slots = couple.shape[0]
    for at in range(0, width, 512):
        mask[:slots, at : at + 512] = listed_mask(couple, base + at // rank, 512, rank)

    def fill(q, carry):
        begin = pl.multiple_of(q * group, LANES)
        target = pl.multiple_of(begin + 2 * group, LANES)
        fill_block(
            src, tgt, begin, target, 5 * group, mask[:, pl.ds(target, group)], rank,
            high, low, pl.multiple_of(q * 5 * group, LANES),
        )
        return carry

    def use(q, carry):
        begin = pl.multiple_of(q * group, LANES)
        out[:, pl.ds(pl.multiple_of(begin + 2 * group, LANES), group)] = use_block(
            coef, begin, 5 * group, high, low, pl.multiple_of(q * 5 * group, LANES)
        )
        return carry

    count = width // group - 4
    lax.fori_loop(0, count, fill, 0, unroll=unroll)
    lax.fori_loop(0, count, use, 0, unroll=unroll)
    span = FAN * leaf
    for g in range(basis.shape[1] // span):
        rows = slice(g * group, (g + 1) * group)
        big_high[rows, :], big_low[rows, :] = block_rows(basis, g * span, leaf)


def edge_kernel(
    device, first, second, c3, c2, rhs, points, near, couple,
    near_edge, g3_edge, g2, ext, src, tgt, coef, high, low,
    *, leaf, rank, starts,
):
    group = FAN * rank
    rim = 2 * group
    halo = REACH * leaf
    vectors = rhs.shape[0]
    n3 = c3.shape[1]
    n2 = c2.shape[1]
    n_points = rhs.shape[1]
    l3 = 0
    r3 = l3 + 3 * rim
    l2 = r3 + 3 * rim
    ln = l2 + n2 + 2 * rim
    rn = ln + 3 * halo

    def rims(left, right):
        ext[:, l3 : l3 + rim] = left[:, :rim]
        ext[:, r3 + 2 * rim : r3 + 3 * rim] = right[:, :rim]
        ext[:, l2 : l2 + rim] = left[:, rim : 2 * rim]
        ext[:, l2 + rim + n2 : l2 + 2 * rim + n2] = right[:, rim : 2 * rim]
        ext[:, ln : ln + halo] = left[:, 2 * rim : 2 * rim + halo]
        ext[:, rn + 2 * halo : rn + 3 * halo] = right[:, 2 * rim : 2 * rim + halo]

    @pl.when(device[0] % 2 == 0)
    def _():
        rims(second, first)

    @pl.when(device[0] % 2 == 1)
    def _():
        rims(first, second)

    ext[:, l3 + rim : l3 + 3 * rim] = c3[:, : 2 * rim]
    ext[:, r3 : r3 + 2 * rim] = c3[:, n3 - 2 * rim :]
    ext[:, l2 + rim : l2 + rim + n2] = c2[...]
    for to, begin in ((ln + halo, 0), (rn, n_points - 2 * halo)):
        ext[:vectors, to : to + 2 * halo] = rhs[:, begin : begin + 2 * halo]
        ext[vectors:, to : to + 2 * halo] = pad_rows(points[:, begin : begin + 2 * halo])
    set_features(ext[vectors:, :], src, tgt, 0)
    coef[...] = stack2(ext[:vectors, :])
    base3 = starts[3] - 1
    base2 = starts[2] - 1
    n_leaves = n_points // leaf
    jobs = []
    for i in range(2):
        for to, begin, cluster in ((i, l3, i * FAN), (2 + i, r3, (n3 // group - 2 + i) * FAN)):
            jobs.append((g3_edge, to * group, begin + i * group, 5 * group, rim, base3 + cluster))
    for q in range(n2 // group):
        jobs.append((g2, q * group, l2 + q * group, 5 * group, rim, base2 + q * FAN))
    jobs.append((near_edge, 0, ln, 3 * halo, halo, 0))
    jobs.append((near_edge, halo, rn, 3 * halo, halo, n_leaves - 2))
    at = 0
    for out, to, begin, n_rows, ahead, cluster in jobs:
        if out is near_edge:
            mask, size = near_mask(near, cluster * leaf, halo, leaf), leaf
        else:
            mask, size = listed_mask(couple, cluster, group, rank), rank
        fill_block(src, tgt, begin, begin + ahead, n_rows, mask, size, high, low, at)
        at += n_rows
    at = 0
    for out, to, begin, n_rows, ahead, cluster in jobs:
        out[:, to : to + LANES] = use_block(coef, begin, n_rows, high, low, at)
        at += n_rows


def final_kernel(
    device, gathered, roots, tile0, c1, first, second, third, couple, near, near_edge,
    g3, g3_edge, g2, table_high, table_low, big_high, big_low, out,
    ext, src, tgt, coef, high, low, *, leaf, rank, starts, xor,
):
    group = FAN * rank
    vectors = out.shape[0]
    me = device[0]
    n_roots = roots.shape[1]
    n_all = n_roots * rank
    here = 2 * (2 * group) + REACH * leaf
    block = iota((8, LANES), 1) // rank
    for at in range(0, n_roots, FAN):
        tiles = [jnp.zeros((8, LANES), F32)] * 3
        for j in range(FAN):
            value = gathered[at + j]
            for i in range(3):
                turn = ((j - i) % FAN) * rank
                turned = pltpu.roll(value, turn, 1) if turn else value
                tiles[i] = jnp.where(block == j, turned, tiles[i])
        lanes = slice(at * rank, at * rank + LANES)
        for i in range(3):
            ext[8 * i : 8 * i + 8, lanes] = tiles[i]
    one = n_all

    def order(parts):
        for i, part in enumerate(parts):
            ext[:, one + i * group : one + (i + 1) * group] = part

    own = first[:, here : here + group]
    near_by = second[:, here : here + group]
    beyond = second[:, here + group : here + 2 * group]

    @pl.when(me % 2 == 0)
    def _():
        order((beyond, near_by, c1[...], own, third[...]))

    @pl.when(me % 2 == 1)
    def _():
        order((third[...], own, c1[...], near_by, beyond))

    root = one + 5 * group
    ext[vectors:, root : root + LANES] = pltpu.roll(tile0[...], rank, 1)
    ext[:vectors, root : root + LANES] = jnp.zeros((vectors, LANES), F32)
    set_features(ext[vectors:, :root], src, None, 0)
    set_features(ext[vectors:, one + 2 * group : one + 3 * group], None, tgt, 0)
    set_features(ext[vectors:, root : root + LANES], None, tgt, LANES)
    listed = (jnp.broadcast_to(roots[...], (8, n_roots)) >= 0).astype(F32).astype(BF16)
    for at in range(0, n_all, 512):
        shape = (n_roots, 512)
        source = at // rank + iota(shape, 1) // rank
        if xor:
            source = jnp.bitwise_xor(source, me)
        usable = dot(listed, (iota(shape, 0) == source).astype(F32).astype(BF16))
        coef[:, at : at + 512] = stack2(ext[:vectors, at : at + 512] * usable[0:1])
    coef[:, one:root] = stack2(ext[:vectors, one:root])
    for at in range(0, n_all, 512):
        fill_block(src, tgt, at, LANES, 512, None, rank, high, low, at)
    fill_block(
        src, tgt, one, 0, 5 * group, listed_mask(couple, 0, group, rank), rank, high, low, one
    )
    f0 = jnp.zeros((vectors, LANES), F32)
    for at in range(0, n_all, 512):
        f0 = f0 + use_block(coef, at, 512, high, low, at)
    g1 = use_block(coef, one, 5 * group, high, low, one)

    def down(above, level, q):
        begin = (starts[level] - 1) * rank + q * group
        rows = slice(begin, begin + group)
        return dot2(above, table_high[rows, :], table_low[rows, :], NT)

    f1 = stack2(g1 + down(stack2(f0), 1, 0))
    f2 = []
    for q in range(FAN):
        f2.append(stack2(g2[:, q * group : (q + 1) * group] + down(f1, 2, q)))
    count = FAN * FAN
    span = FAN * leaf
    halo = REACH * leaf
    for q in range(count):
        if q < 2:
            total = g3_edge[:, q * group : (q + 1) * group]
        elif q >= count - 2:
            to = (q - count + 4) * group
            total = g3_edge[:, to : to + group]
        else:
            total = g3[:, q * group : (q + 1) * group]
        f3 = stack2(total + down(f2[q // FAN], 3, q))
        rows = slice(q * group, (q + 1) * group)
        value = dot2(f3, big_high[rows, :], big_low[rows, :])
        if q == 0:
            base = jnp.concatenate([near_edge[:, :halo], near[:, halo:span]], axis=1)
        elif q == count - 1:
            base = jnp.concatenate(
                [near[:, q * span : (q + 1) * span - halo], near_edge[:, halo:]], axis=1
            )
        else:
            base = near[:, q * span : (q + 1) * span]
        out[:, q * span : (q + 1) * span] = base + value


def largest_unroll(count, most):
    return max(d for d in range(1, most + 1) if count % d == 0)


def body(points, rhs, leaf_basis, transfer, proxies, near_list, couple_list, root_list):
    count = lax.axis_size("leaf")
    device = lax.axis_index("leaf").astype(jnp.int32)[None]
    rank = leaf_basis.shape[0]
    vectors, n_points = rhs.shape
    n_leaves = near_list.shape[0]
    leaf = n_points // n_leaves
    group = FAN * rank
    rim = 2 * group
    halo = REACH * leaf
    starts = [(FAN**level - 1) // (FAN - 1) for level in range(LEVELS + 1)]
    n_clusters = transfer.shape[2]
    n3 = FAN**3 * rank
    n2 = FAN**2 * rank
    flat_transfer = transfer.reshape(rank * rank, n_clusters)
    flat_prox = proxies.reshape(proxies.shape[0] * rank, proxies.shape[2])
    near_t = near_list.T
    couple_t = couple_list.T

    vmem = pl.BlockSpec(memory_space=pltpu.VMEM)
    smem = pl.BlockSpec(memory_space=pltpu.SMEM)

    def shape(*dims, dtype=F32):
        return jax.ShapeDtypeStruct(dims, dtype)

    def call(kernel, n_in, outs, scratch, name, mib, scalar=True):
        return pl.pallas_call(
            kernel,
            out_shape=outs,
            in_specs=([smem] if scalar else []) + [vmem] * n_in,
            out_specs=jax.tree.map(lambda _: vmem, outs),
            scratch_shapes=scratch,
            compiler_params=pltpu.CompilerParams(vmem_limit_bytes=mib << 20),
            name=name,
        )

    padded_clusters = -(-n_clusters // 8) * 8
    width = 2 * rim + halo + group
    c3, c2, c1, tile0, to_first, to_second, table_high, table_low = call(
        lambda *refs: upward_kernel(*refs, leaf=leaf, rank=rank, starts=starts),
        5,
        (
            shape(ROWS, n3),
            shape(ROWS, n2),
            shape(ROWS, group),
            shape(8, LANES),
            shape(ROWS, width + LANES),
            shape(ROWS, width),
            shape(n_clusters * rank, LANES, dtype=BF16),
            shape(n_clusters * rank, LANES, dtype=BF16),
        ),
        [pltpu.VMEM((rank * rank, LANES), F32), pltpu.VMEM((padded_clusters, rank, LANES), F32)],
        "upward",
        16,
    )(device, rhs, points, leaf_basis, flat_transfer, flat_prox)

    def swap(value, step):
        return lax.ppermute(value, "leaf", [(i, i ^ step) for i in range(count)])

    first = swap(to_first, 1)
    send, gathered = call(
        middle_kernel,
        3,
        (shape(ROWS, width + group), shape(2, 8, LANES)),
        [],
        "middle",
        2,
        scalar=False,
    )(first, to_second, tile0)
    xor = count & (count - 1) == 0

    def join(lower, upper):
        return call(
            join_kernel, 2, shape(2 * lower.shape[0], 8, LANES), [], "join", 2, scalar=False
        )(lower, upper)

    if xor:
        step = 2
        while step < count:
            other = swap(gathered, step)
            if step == 2:
                pairs = [(i, i + 1) for i in range(1, count - 1, 2)]
                second = lax.ppermute(send, "leaf", pairs + [(j, i) for i, j in pairs])
                third = swap(second[:, width - group : width], 1)
            gathered = join(gathered, other)
            step *= 2
    else:
        gathered = lax.all_gather(tile0, "leaf", axis=0)
        pairs = [(i, i + 1) for i in range(1, count - 1, 2)]
        second = lax.ppermute(send, "leaf", pairs + [(j, i) for i, j in pairs])
        third = swap(second[:, width - group : width], 1)

    n_near = n_points // halo - 2
    near = call(
        lambda *refs: near_kernel(*refs, leaf=leaf, unroll=largest_unroll(n_near, 16)),
        3,
        shape(vectors, n_points),
        [
            pltpu.VMEM((n_points, FEATS), BF16),
            pltpu.VMEM((FEATS, n_points), BF16),
            pltpu.VMEM((2 * vectors, n_points), BF16),
            pltpu.VMEM((8, n_points), F32),
            pltpu.VMEM((n_near * 3 * halo, LANES), BF16),
            pltpu.VMEM((n_near * 3 * halo, LANES), BF16),
        ],
        "near",
        16,
        scalar=False,
    )(rhs, points, near_t)

    n_far = FAN**2 - 4
    span = FAN * leaf
    g3, big_high, big_low = call(
        lambda *refs: far_kernel(
            *refs, leaf=leaf, rank=rank, base=starts[3] - 1, unroll=largest_unroll(n_far, 12)
        ),
        3,
        (
            shape(vectors, n3),
            shape(n_points // span * group, span, dtype=BF16),
            shape(n_points // span * group, span, dtype=BF16),
        ),
        [
            pltpu.VMEM((n3, FEATS), BF16),
            pltpu.VMEM((FEATS, n3), BF16),
            pltpu.VMEM((2 * vectors, n3), BF16),
            pltpu.VMEM((ROWS, n3), F32),
            pltpu.VMEM((n_far * 5 * group, LANES), BF16),
            pltpu.VMEM((n_far * 5 * group, LANES), BF16),
        ],
        "far",
        16,
        scalar=False,
    )(c3, couple_t, leaf_basis)

    n_ext = 6 * rim + n2 + 2 * rim + 6 * halo
    n_rows = (4 + n2 // group) * 5 * group + 2 * 3 * halo
    near_edge, g3_edge, g2 = call(
        lambda *refs: edge_kernel(*refs, leaf=leaf, rank=rank, starts=starts),
        8,
        (shape(vectors, 2 * halo), shape(vectors, 2 * rim), shape(vectors, n2)),
        [
            pltpu.VMEM((ROWS, n_ext), F32),
            pltpu.VMEM((n_ext, FEATS), BF16),
            pltpu.VMEM((FEATS, n_ext), BF16),
            pltpu.VMEM((2 * vectors, n_ext), BF16),
            pltpu.VMEM((n_rows, LANES), BF16),
            pltpu.VMEM((n_rows, LANES), BF16),
        ],
        "edge",
        16,
    )(device, first, second, c3, c2, rhs, points, near_t, couple_t)

    n_all = count * rank
    n_top = n_all + 5 * group
    return call(
        lambda *refs: final_kernel(*refs, leaf=leaf, rank=rank, starts=starts, xor=xor),
        17,
        shape(vectors, n_points),
        [
            pltpu.VMEM((ROWS, n_top + LANES), F32),
            pltpu.VMEM((n_top, FEATS), BF16),
            pltpu.VMEM((FEATS, 2 * LANES), BF16),
            pltpu.VMEM((2 * vectors, n_top), BF16),
            pltpu.VMEM((n_top, LANES), BF16),
            pltpu.VMEM((n_top, LANES), BF16),
        ],
        "final",
        16,
    )(
        device, gathered, root_list, tile0, c1, first, second, third, couple_t, near, near_edge,
        g3, g3_edge, g2, table_high, table_low, big_high, big_low,
    )


def solution(mesh):
    in_specs = (
        P(None, "leaf"),
        P(None, "leaf"),
        P(None, "leaf"),
        P(None, None, "leaf"),
        P(None, None, "leaf"),
        P("leaf", None),
        P("leaf", None),
        P("leaf", None),
    )
    out_specs = P(None, "leaf")
    return jax.shard_map(body, mesh=mesh, in_specs=in_specs, out_specs=out_specs, check_vma=False)
```

```python
import math

import jax
import jax.numpy as jnp
from jax import lax
from jax.experimental import pallas as pl
from jax.experimental.pallas import tpu as pltpu
from jax.sharding import PartitionSpec as P


LEVELS = 3
REACH = 2
FAN = 4
LANES = 128
ROWS = 24
FEATS = 32
SCALE = 10.0 * math.log2(math.e)
F32 = jnp.float32
BF16 = jnp.bfloat16

NN = (((1,), (0,)), ((), ()))
NT = (((1,), (1,)), ((), ()))


def dot(lhs, rhs, dims=NN):
    return lax.dot_general(lhs, rhs, dims, preferred_element_type=F32)


def iota(shape, axis):
    return lax.broadcasted_iota(jnp.int32, shape, axis)


def split2(value):
    high = value.astype(BF16)
    low = (value - high.astype(F32)).astype(BF16)
    return high, low


def split3(value):
    high = value.astype(BF16).astype(F32)
    rest = value - high
    mid = rest.astype(BF16).astype(F32)
    return high, mid, rest - mid


def stack2(value):
    high, low = split2(value)
    return jnp.concatenate([high, low], axis=0)


def dot2(both, high, low, dims=NN):
    rows = both.shape[0] // 2
    wide = dot(both, high, dims)
    return wide[:rows] + wide[rows:] + dot(both[:rows], low, dims)


def spread(clusters, width, begin, size):
    shape = (clusters, width)
    return (iota(shape, 0) == begin + iota(shape, 1) // size).astype(BF16)


def listed_mask(lists, begin, width, size):
    listed = (lists[...] >= 0).astype(F32).astype(BF16)
    return dot(listed, spread(lists.shape[1], width, begin, size))


def block_rows(basis, offset, leaf):
    part = basis[:, offset : offset + FAN * leaf]
    rank = part.shape[0]
    tiled = jnp.concatenate([part] * FAN, axis=0)
    keep = iota(tiled.shape, 0) // rank == iota(tiled.shape, 1) // leaf
    return split2(jnp.where(keep, tiled, 0.0))


def pick(groups):
    shape = (FEATS, FEATS)
    feature = iota(shape, 0)
    want = jnp.full(shape, -1, jnp.int32)
    for g, row in enumerate(groups):
        want = jnp.where(feature // 3 == g, row + feature % 3, want)
    return (iota(shape, 1) == want).astype(F32).astype(BF16)


def features(position):
    row = iota(position.shape, 0)
    centred = jnp.where(row < 3, position - 0.5, 0.0)
    norm = -SCALE * jnp.sum(centred * centred, axis=0, keepdims=True)
    tail = jnp.where((row >= 3) & (row < 6), 1.0, 0.0)
    for r, part in enumerate(split3(norm)):
        tail = jnp.where(row == r, part, tail)
    own = jnp.concatenate([*split3(centred), tail], axis=0).astype(BF16)
    other = jnp.concatenate([*split3(centred * (2.0 * SCALE)), tail], axis=0).astype(BF16)
    source = dot(pick((0, 0, 0, 8, 8, 16, 24, 27)), own)
    target = dot(pick((0, 8, 16, 0, 8, 0, 27, 24)), other)
    return source, target


def set_features(position, src, tgt, begin):
    n = position.shape[1]
    for at in range(0, n, 512):
        end = min(at + 512, n)
        source, target = features(position[:, at:end])
        if tgt is not None:
            tgt[:, begin + at : begin + end] = target.astype(BF16)
        if src is not None:
            for lane in range(0, end - at, LANES):
                to = begin + at + lane
                src[to : to + LANES, :] = jnp.transpose(source[:, lane : lane + LANES]).astype(
                    BF16
                )


def pad_rows(points):
    return jnp.concatenate([points, jnp.zeros((8 - points.shape[0], points.shape[1]), F32)], axis=0)


def fill_block(src, tgt, row, lane, n_rows, mask, size, high, low, at):
    kernel = jnp.exp2(dot(src[pl.ds(row, n_rows), :], tgt[:, pl.ds(lane, LANES)]))
    if mask is not None:
        kernel = jnp.concatenate(
            [kernel[size * s : size * (s + 1)] * mask[s : s + 1] for s in range(n_rows // size)],
            axis=0,
        )
    high[pl.ds(at, n_rows), :], low[pl.ds(at, n_rows), :] = split2(kernel)


def use_block(coef, row, n_rows, high, low, at):
    return dot2(coef[:, pl.ds(row, n_rows)], high[pl.ds(at, n_rows), :], low[pl.ds(at, n_rows), :])


def upward_kernel(
    device, rhs_hbm, points_hbm, basis_hbm, transfer_hbm, prox_hbm,
    c3, c2, c1, tile0, first, second, table_high, table_low,
    rhs, points, basis, transfer, prox, padded, moved, sems, *, leaf, rank, starts,
):
    vectors = rhs.shape[0]
    coords = points.shape[0]
    span = FAN * leaf
    group = FAN * rank
    outs = {1: c1, 2: c2, 3: c3}
    copies = [
        pltpu.make_async_copy(source, to, sems.at[i])
        for i, (source, to) in enumerate(
            (
                (transfer_hbm, transfer),
                (basis_hbm, basis),
                (rhs_hbm, rhs),
                (prox_hbm, prox),
                (points_hbm, points),
            )
        )
    ]
    for copy in copies:
        copy.start()
    copies[0].wait()

    n_clusters = transfer.shape[1]
    padded[...] = jnp.zeros(padded.shape, F32)
    padded[:, :n_clusters] = transfer[...]
    row = iota((8, LANES), 0)
    block = iota((8, LANES), 1) // rank
    for a in range(0, rank, FAN):
        flipped = jnp.transpose(padded[a * rank : (a + FAN) * rank, :])
        for t in range(0, n_clusters, 8):
            tile = flipped[t : t + 8]
            turns = [tile] + [pltpu.roll(tile, rank * s, 1) for s in range(1, FAN)]
            low = (t // FAN - 1) % FAN
            up = (t // FAN) % FAN
            in_low = (row < FAN) & (block == low)
            in_up = (row >= FAN) & (block == up)
            for j in range(FAN):
                value = jnp.where(in_up, turns[(up - j) % FAN], 0.0)
                value = jnp.where(in_low, turns[(low - j) % FAN], value)
                moved[t : t + 8, a + j, :] = value
    for t in range(0, n_clusters, FAN):
        rows = slice(t * rank, t * rank + group)
        table_high[rows, :], table_low[rows, :] = split2(
            moved[t : t + FAN].reshape(group, LANES)
        )

    for copy in copies[1:]:
        copy.wait()
    for g in range(rhs.shape[1] // span):
        high, low = block_rows(basis, g * span, leaf)
        c3[:vectors, g * group : (g + 1) * group] = dot2(
            stack2(rhs[:, g * span : (g + 1) * span]), high, low, NT
        )
    for level in range(LEVELS, 0, -1):
        source = outs[level]
        count = FAN ** (level - 1)
        base = (starts[level] - 1) * rank
        per = min(FAN, count)
        width = per * group
        for h in range(count // per):
            begin = h * width
            rows = slice(base + begin, base + begin + width)
            merged = dot2(
                stack2(source[:vectors, begin : begin + width]),
                table_high[rows, :],
                table_low[rows, :],
            )
            if level > 1:
                outs[level - 1][:vectors, h * group : (h + 1) * group] = merged
            else:
                root = merged

    parts = jnp.concatenate(split3(prox[...]), axis=0).astype(BF16)
    clusters = prox.shape[1]
    n = coords * rank
    row = iota((8, LANES), 0)
    for level in range(LEVELS + 1):
        total = max(FAN**level * rank, LANES)
        step = min(total, 512)
        for begin in range(0, total, step):
            lines = dot(parts, spread(clusters, step, starts[level] + begin // rank, rank))
            lines = lines[:n] + lines[n : 2 * n] + lines[2 * n :]
            lines = jnp.where(iota(lines.shape, 0) % rank == iota(lines.shape, 1) % rank, lines, 0.0)
            rows = iota((8, step), 0)
            place = jnp.zeros((8, step), F32)
            for c in range(coords):
                line = jnp.sum(lines[c * rank : (c + 1) * rank], axis=0, keepdims=True)
                place = jnp.where(rows == c, line, place)
            if level == 0:
                root_place = place
            else:
                outs[level][vectors:, begin : begin + step] = place
    last = (FAN - 1) * rank
    tile = jnp.where(block == 0, pltpu.roll(root[:8], LANES - last, 1), 0.0)
    tile = jnp.where(block == 1, pltpu.roll(root[8:16], LANES - last + rank, 1), tile)
    tile = jnp.where(block == 2, pltpu.roll(root_place, 2 * rank, 1), tile)
    tile0[...] = tile

    rim = 2 * group
    halo = REACH * leaf

    def fill(send, tail):
        at = 0
        for ref, width in ((c3, rim), (c2, rim)):
            begin = ref.shape[1] - width if tail else 0
            send[:, at : at + width] = ref[:, begin : begin + width]
            at += width
        begin = points.shape[1] - halo if tail else 0
        send[:vectors, at : at + halo] = rhs[:, begin : begin + halo]
        send[vectors:, at : at + halo] = pad_rows(points[:, begin : begin + halo])

    @pl.when(device[0] % 2 == 0)
    def _():
        fill(first, True)
        fill(second, False)

    @pl.when(device[0] % 2 == 1)
    def _():
        fill(first, False)
        fill(second, True)

    at = 2 * rim + halo
    first[:, at : at + group] = c1[...]
    second[:, at : at + group] = c1[...]
    first[:8, at + group :] = tile
    first[8:, at + group :] = jnp.zeros((ROWS - 8, LANES), F32)


def middle_kernel(first, second, tile0, send, pair):
    width = second.shape[1]
    send[:, :width] = second[...]
    send[:, width:] = first[:, width - LANES : width]
    pair[0] = tile0[...]
    pair[1] = first[:8, width:]


def join_kernel(lower, upper, out):
    count = lower.shape[0]
    out[:count] = lower[...]
    out[count:] = upper[...]


def near_kernel(rhs, points, near, out, src, tgt, coef, mask, high, low, *, leaf, begin, unroll):
    halo = REACH * leaf
    width = coef.shape[1]
    count = width // halo - 2
    lanes = slice(begin * halo, begin * halo + width)
    set_features(pad_rows(points[:, lanes]), src, tgt, 0)
    coef[...] = stack2(rhs[:, lanes])
    for at in range(0, width, 512):
        end = min(at + 512, width)
        mask[:, at:end] = near_mask(near, begin * halo + at, end - at, leaf)

    def fill(g, carry):
        row = pl.multiple_of(g * halo, LANES)
        target = pl.multiple_of(row + halo, LANES)
        fill_block(
            src, tgt, row, target, 3 * halo, mask[:, pl.ds(target, halo)], leaf,
            high, low, pl.multiple_of(g * 3 * halo, LANES),
        )
        return carry

    def use(g, carry):
        row = pl.multiple_of(g * halo, LANES)
        out[:, pl.ds(row, halo)] = use_block(
            coef, row, 3 * halo, high, low, pl.multiple_of(g * 3 * halo, LANES)
        )
        return carry

    lax.fori_loop(0, count, fill, 0, unroll=unroll)
    lax.fori_loop(0, count, use, 0, unroll=unroll)


def near_mask(near, begin, width, leaf):
    rows = listed_mask(near, begin // leaf, width, leaf)
    slots = rows.shape[0]
    odd = (iota((8, width), 1) // leaf) % 2 == 1
    even_rows = jnp.concatenate([rows, jnp.zeros((8 - slots, width), F32)], axis=0)
    return jnp.where(odd, pltpu.roll(even_rows, 1, 0), even_rows)


def far_kernel(
    device, c3, couple, basis, roots, out, big_high, big_low, usable,
    src, tgt, coef, mask, high, low, *, leaf, rank, base, unroll, xor,
):
    group = FAN * rank
    vectors = out.shape[0]
    width = c3.shape[1]
    set_features(c3[vectors:, :], src, tgt, 0)
    coef[...] = stack2(c3[:vectors, :])
    slots = couple.shape[0]
    for at in range(0, width, 512):
        mask[:slots, at : at + 512] = listed_mask(couple, base + at // rank, 512, rank)

    def fill(q, carry):
        begin = pl.multiple_of(q * group, LANES)
        target = pl.multiple_of(begin + 2 * group, LANES)
        fill_block(
            src, tgt, begin, target, 5 * group, mask[:, pl.ds(target, group)], rank,
            high, low, pl.multiple_of(q * 5 * group, LANES),
        )
        return carry

    def use(q, carry):
        begin = pl.multiple_of(q * group, LANES)
        out[:, pl.ds(pl.multiple_of(begin + 2 * group, LANES), group)] = use_block(
            coef, begin, 5 * group, high, low, pl.multiple_of(q * 5 * group, LANES)
        )
        return carry

    count = width // group - 4
    lax.fori_loop(0, count, fill, 0, unroll=unroll)
    lax.fori_loop(0, count, use, 0, unroll=unroll)
    span = FAN * leaf
    for g in range(basis.shape[1] // span):
        rows = slice(g * group, (g + 1) * group)
        big_high[rows, :], big_low[rows, :] = block_rows(basis, g * span, leaf)
    n_roots = roots.shape[1]
    listed = (jnp.broadcast_to(roots[...], (8, n_roots)) >= 0).astype(F32).astype(BF16)
    for at in range(0, n_roots * rank, 512):
        shape = (n_roots, 512)
        source = at // rank + iota(shape, 1) // rank
        if xor:
            source = jnp.bitwise_xor(source, device[0])
        usable[:, at : at + 512] = dot(listed, (iota(shape, 0) == source).astype(F32).astype(BF16))


def edge_kernel(
    device, first, second, third, c3, c2, c1, rhs, points, near, couple,
    near_edge, g3_edge, g2, g1, ext, src, tgt, coef, high, low,
    *, leaf, rank, starts,
):
    group = FAN * rank
    rim = 2 * group
    halo = REACH * leaf
    vectors = rhs.shape[0]
    n3 = c3.shape[1]
    n2 = c2.shape[1]
    n_points = rhs.shape[1]
    l3 = 0
    r3 = l3 + 3 * rim
    l2 = r3 + 3 * rim
    ln = l2 + n2 + 2 * rim
    rn = ln + 3 * halo
    one = rn + 3 * halo
    here = 2 * rim + halo
    own = first[:, here : here + group]
    near_by = second[:, here : here + group]
    beyond = second[:, here + group : here + 2 * group]

    def rims(left, right, parts):
        for i, part in enumerate(parts):
            ext[:, one + i * group : one + (i + 1) * group] = part
        ext[:, l3 : l3 + rim] = left[:, :rim]
        ext[:, r3 + 2 * rim : r3 + 3 * rim] = right[:, :rim]
        ext[:, l2 : l2 + rim] = left[:, rim : 2 * rim]
        ext[:, l2 + rim + n2 : l2 + 2 * rim + n2] = right[:, rim : 2 * rim]
        ext[:, ln : ln + halo] = left[:, 2 * rim : 2 * rim + halo]
        ext[:, rn + 2 * halo : rn + 3 * halo] = right[:, 2 * rim : 2 * rim + halo]

    @pl.when(device[0] % 2 == 0)
    def _():
        rims(second, first, (beyond, near_by, c1[...], own, third[...]))

    @pl.when(device[0] % 2 == 1)
    def _():
        rims(first, second, (third[...], own, c1[...], near_by, beyond))

    ext[:, l3 + rim : l3 + 3 * rim] = c3[:, : 2 * rim]
    ext[:, r3 : r3 + 2 * rim] = c3[:, n3 - 2 * rim :]
    ext[:, l2 + rim : l2 + rim + n2] = c2[...]
    for to, begin in ((ln + halo, 0), (rn, n_points - 2 * halo)):
        ext[:vectors, to : to + 2 * halo] = rhs[:, begin : begin + 2 * halo]
        ext[vectors:, to : to + 2 * halo] = pad_rows(points[:, begin : begin + 2 * halo])
    set_features(ext[vectors:, :], src, tgt, 0)
    coef[...] = stack2(ext[:vectors, :])
    base3 = starts[3] - 1
    base2 = starts[2] - 1
    n_leaves = n_points // leaf
    jobs = []
    for i in range(2):
        for to, begin, cluster in ((i, l3, i * FAN), (2 + i, r3, (n3 // group - 2 + i) * FAN)):
            jobs.append((g3_edge, to * group, begin + i * group, 5 * group, rim, base3 + cluster))
    for q in range(n2 // group):
        jobs.append((g2, q * group, l2 + q * group, 5 * group, rim, base2 + q * FAN))
    jobs.append((g1, 0, one, 5 * group, rim, starts[1] - 1))
    jobs.append((near_edge, 0, ln, 3 * halo, halo, 0))
    jobs.append((near_edge, halo, rn, 3 * halo, halo, n_leaves - 2))
    at = 0
    for out, to, begin, n_rows, ahead, cluster in jobs:
        if out is near_edge:
            mask, size = near_mask(near, cluster * leaf, halo, leaf), leaf
        else:
            mask, size = listed_mask(couple, cluster, group, rank), rank
        fill_block(src, tgt, begin, begin + ahead, n_rows, mask, size, high, low, at)
        at += n_rows
    at = 0
    for out, to, begin, n_rows, ahead, cluster in jobs:
        out[:, to : to + LANES] = use_block(coef, begin, n_rows, high, low, at)
        at += n_rows


def final_kernel(
    gathered, usable, tile0, near_low, near_high, near_edge, g3, g3_edge, g2, g1,
    table_high, table_low, big_high, big_low, out,
    ext, src, tgt, coef, high, low, *, leaf, rank, starts,
):
    group = FAN * rank
    vectors = out.shape[0]
    n_all = usable.shape[1]
    block = iota((8, LANES), 1) // rank
    for at in range(0, n_all // rank, FAN):
        tiles = [jnp.zeros((8, LANES), F32)] * 3
        for j in range(FAN):
            value = gathered[at + j]
            for i in range(3):
                turn = ((j - i) % FAN) * rank
                turned = pltpu.roll(value, turn, 1) if turn else value
                tiles[i] = jnp.where(block == j, turned, tiles[i])
        lanes = slice(at * rank, at * rank + LANES)
        for i in range(3):
            ext[8 * i : 8 * i + 8, lanes] = tiles[i]
    set_features(ext[vectors:, :], src, None, 0)
    set_features(pltpu.roll(tile0[...], rank, 1), None, tgt, 0)
    for at in range(0, n_all, 512):
        coef[:, at : at + 512] = stack2(
            ext[:vectors, at : at + 512] * usable[0:1, at : at + 512]
        )
        fill_block(src, tgt, at, 0, 512, None, rank, high, low, at)
    f0 = jnp.zeros((vectors, LANES), F32)
    for at in range(0, n_all, 512):
        f0 = f0 + use_block(coef, at, 512, high, low, at)

    def down(above, level, q):
        begin = (starts[level] - 1) * rank + q * group
        rows = slice(begin, begin + group)
        return dot2(above, table_high[rows, :], table_low[rows, :], NT)

    f1 = stack2(g1[...] + down(stack2(f0), 1, 0))
    f2 = []
    for q in range(FAN):
        f2.append(stack2(g2[:, q * group : (q + 1) * group] + down(f1, 2, q)))
    count = FAN * FAN
    span = FAN * leaf
    halo = REACH * leaf
    for q in range(count):
        if q < 2:
            total = g3_edge[:, q * group : (q + 1) * group]
        elif q >= count - 2:
            to = (q - count + 4) * group
            total = g3_edge[:, to : to + group]
        else:
            total = g3[:, q * group : (q + 1) * group]
        f3 = stack2(total + down(f2[q // FAN], 3, q))
        rows = slice(q * group, (q + 1) * group)
        value = dot2(f3, big_high[rows, :], big_low[rows, :])
        out[:, q * span : (q + 1) * span] = value
    n_low = near_low.shape[1]
    n_high = near_high.shape[1]
    out[:, :halo] += near_edge[:, :halo]
    out[:, halo : halo + n_low] += near_low[...]
    out[:, halo + n_low : halo + n_low + n_high] += near_high[...]
    out[:, halo + n_low + n_high :] += near_edge[:, halo:]


def largest_unroll(count, most):
    return max(d for d in range(1, most + 1) if count % d == 0)


def body(points, rhs, leaf_basis, transfer, proxies, near_list, couple_list, root_list):
    count = lax.axis_size("leaf")
    device = lax.axis_index("leaf").astype(jnp.int32)[None]
    rank = leaf_basis.shape[0]
    vectors, n_points = rhs.shape
    n_leaves = near_list.shape[0]
    leaf = n_points // n_leaves
    group = FAN * rank
    rim = 2 * group
    halo = REACH * leaf
    starts = [(FAN**level - 1) // (FAN - 1) for level in range(LEVELS + 1)]
    n_clusters = transfer.shape[2]
    n3 = FAN**3 * rank
    n2 = FAN**2 * rank
    flat_transfer = transfer.reshape(rank * rank, n_clusters)
    flat_prox = proxies.reshape(proxies.shape[0] * rank, proxies.shape[2])
    near_t = near_list.T
    couple_t = couple_list.T

    vmem = pl.BlockSpec(memory_space=pltpu.VMEM)
    smem = pl.BlockSpec(memory_space=pltpu.SMEM)

    def shape(*dims, dtype=F32):
        return jax.ShapeDtypeStruct(dims, dtype)

    def call(kernel, n_in, outs, scratch, mib, scalar=True, space=vmem):
        return pl.pallas_call(
            kernel,
            out_shape=outs,
            in_specs=([smem] if scalar else []) + [space] * n_in,
            out_specs=jax.tree.map(lambda _: vmem, outs),
            scratch_shapes=scratch,
            compiler_params=pltpu.CompilerParams(vmem_limit_bytes=mib << 20),
        )

    padded_clusters = -(-n_clusters // 8) * 8
    width = 2 * rim + halo + group
    c3, c2, c1, tile0, to_first, to_second, table_high, table_low = call(
        lambda *refs: upward_kernel(*refs, leaf=leaf, rank=rank, starts=starts),
        5,
        (
            shape(ROWS, n3),
            shape(ROWS, n2),
            shape(ROWS, group),
            shape(8, LANES),
            shape(ROWS, width + LANES),
            shape(ROWS, width),
            shape(n_clusters * rank, LANES, dtype=BF16),
            shape(n_clusters * rank, LANES, dtype=BF16),
        ),
        [
            *(
                pltpu.VMEM(array.shape, F32)
                for array in (rhs, points, leaf_basis, flat_transfer, flat_prox)
            ),
            pltpu.VMEM((rank * rank, LANES), F32),
            pltpu.VMEM((padded_clusters, rank, LANES), F32),
            pltpu.SemaphoreType.DMA((5,)),
        ],
        16,
        space=pl.BlockSpec(memory_space=pltpu.HBM),
    )(
        device,
        *(
            pltpu.with_memory_space_constraint(array, pltpu.HBM)
            for array in (rhs, points, leaf_basis, flat_transfer, flat_prox)
        ),
    )

    def swap(value, step):
        return lax.ppermute(value, "leaf", [(i, i ^ step) for i in range(count)])

    first = swap(to_first, 1)
    send, gathered = call(
        middle_kernel, 3, (shape(ROWS, width + group), shape(2, 8, LANES)), [], 2, scalar=False
    )(first, to_second, tile0)
    xor = count & (count - 1) == 0

    def join(lower, upper):
        return call(
            join_kernel, 2, shape(2 * lower.shape[0], 8, LANES), [], 2, scalar=False
        )(lower, upper)

    pairs = [(i, i + 1) for i in range(1, count - 1, 2)]
    second = lax.ppermute(send, "leaf", pairs + [(j, i) for i, j in pairs])
    third = swap(second[:, width - group : width], 1)
    if xor:
        step = 2
        while step < count:
            other = swap(gathered, step)
            gathered = join(gathered, other)
            step *= 2
    else:
        gathered = lax.all_gather(tile0, "leaf", axis=0)

    n_groups = n_points // halo

    def near_part(begin, n_near):
        lanes = (n_near + 2) * halo
        return call(
            lambda *refs: near_kernel(
                *refs, leaf=leaf, begin=begin, unroll=largest_unroll(n_near, 16)
            ),
            3,
            shape(vectors, n_near * halo),
            [
                pltpu.VMEM((lanes, FEATS), BF16),
                pltpu.VMEM((FEATS, lanes), BF16),
                pltpu.VMEM((2 * vectors, lanes), BF16),
                pltpu.VMEM((8, lanes), F32),
                pltpu.VMEM((n_near * 3 * halo, LANES), BF16),
                pltpu.VMEM((n_near * 3 * halo, LANES), BF16),
            ],
            12,
            scalar=False,
        )(rhs, points, near_t)

    half = (n_groups - 2) // 2
    near_low = near_part(0, half)
    near_high = near_part(half, n_groups - 2 - half)

    n_all = count * rank
    n_far = FAN**2 - 4
    span = FAN * leaf
    g3, big_high, big_low, usable = call(
        lambda *refs: far_kernel(
            *refs, leaf=leaf, rank=rank, base=starts[3] - 1, unroll=largest_unroll(n_far, 12),
            xor=xor,
        ),
        4,
        (
            shape(vectors, n3),
            shape(n_points // span * group, span, dtype=BF16),
            shape(n_points // span * group, span, dtype=BF16),
            shape(8, n_all),
        ),
        [
            pltpu.VMEM((n3, FEATS), BF16),
            pltpu.VMEM((FEATS, n3), BF16),
            pltpu.VMEM((2 * vectors, n3), BF16),
            pltpu.VMEM((ROWS, n3), F32),
            pltpu.VMEM((n_far * 5 * group, LANES), BF16),
            pltpu.VMEM((n_far * 5 * group, LANES), BF16),
        ],
        12,
    )(device, c3, couple_t, leaf_basis, root_list)

    n_ext = 6 * rim + n2 + 2 * rim + 6 * halo + 5 * group
    n_rows = (5 + n2 // group) * 5 * group + 2 * 3 * halo
    near_edge, g3_edge, g2, g1 = call(
        lambda *refs: edge_kernel(*refs, leaf=leaf, rank=rank, starts=starts),
        10,
        (
            shape(vectors, 2 * halo),
            shape(vectors, 2 * rim),
            shape(vectors, n2),
            shape(vectors, group),
        ),
        [
            pltpu.VMEM((ROWS, n_ext), F32),
            pltpu.VMEM((n_ext, FEATS), BF16),
            pltpu.VMEM((FEATS, n_ext), BF16),
            pltpu.VMEM((2 * vectors, n_ext), BF16),
            pltpu.VMEM((n_rows, LANES), BF16),
            pltpu.VMEM((n_rows, LANES), BF16),
        ],
        12,
    )(
        device, first, second, third, c3, c2, c1, rhs, points, near_t, couple_t,
    )

    return call(
        lambda *refs: final_kernel(*refs, leaf=leaf, rank=rank, starts=starts),
        14,
        shape(vectors, n_points),
        [
            pltpu.VMEM((ROWS, n_all), F32),
            pltpu.VMEM((n_all, FEATS), BF16),
            pltpu.VMEM((FEATS, LANES), BF16),
            pltpu.VMEM((2 * vectors, n_all), BF16),
            pltpu.VMEM((n_all, LANES), BF16),
            pltpu.VMEM((n_all, LANES), BF16),
        ],
        12,
        scalar=False,
    )(
        gathered, usable, tile0, near_low, near_high, near_edge, g3, g3_edge, g2, g1,
        table_high, table_low, big_high, big_low,
    )


def solution(mesh):
    in_specs = (
        P(None, "leaf"),
        P(None, "leaf"),
        P(None, "leaf"),
        P(None, None, "leaf"),
        P(None, None, "leaf"),
        P("leaf", None),
        P("leaf", None),
        P("leaf", None),
    )
    out_specs = P(None, "leaf")
    return jax.shard_map(body, mesh=mesh, in_specs=in_specs, out_specs=out_specs, check_vma=False)
```

```python
import math

import jax
import jax.numpy as jnp
from jax import lax
from jax.experimental import pallas as pl
from jax.experimental.pallas import tpu as pltpu
from jax.sharding import PartitionSpec as P


LEVELS = 3
REACH = 2
FAN = 4
LANES = 128
ROWS = 24
FEATS = 32
SCALE = 10.0 * math.log2(math.e)
F32 = jnp.float32
BF16 = jnp.bfloat16

NN = (((1,), (0,)), ((), ()))
NT = (((1,), (1,)), ((), ()))


def dot(lhs, rhs, dims=NN):
    return lax.dot_general(lhs, rhs, dims, preferred_element_type=F32)


def iota(shape, axis):
    return lax.broadcasted_iota(jnp.int32, shape, axis)


def split2(value):
    high = value.astype(BF16)
    low = (value - high.astype(F32)).astype(BF16)
    return high, low


def split3(value):
    high = value.astype(BF16).astype(F32)
    rest = value - high
    mid = rest.astype(BF16).astype(F32)
    return high, mid, rest - mid


def stack2(value):
    high, low = split2(value)
    return jnp.concatenate([high, low], axis=0)


def dot2(both, high, low, dims=NN):
    rows = both.shape[0] // 2
    wide = dot(both, high, dims)
    return wide[:rows] + wide[rows:] + dot(both[:rows], low, dims)


def spread(clusters, width, begin, size):
    shape = (clusters, width)
    return (iota(shape, 0) == begin + iota(shape, 1) // size).astype(BF16)


def listed_mask(lists, begin, width, size):
    listed = (lists[...] >= 0).astype(F32).astype(BF16)
    return dot(listed, spread(lists.shape[1], width, begin, size))


def block_rows(basis, offset, leaf):
    out = []
    for part in split2(basis[:, offset : offset + FAN * leaf]):
        rank = part.shape[0]
        zero = jnp.zeros((rank, LANES), BF16)
        lane = iota((rank, LANES), 1)
        rows = []
        for t in range(FAN):
            pieces = []
            for begin in range(0, FAN * leaf, LANES):
                first = t * leaf - begin
                if 0 <= first < LANES:
                    keep = ((lane >= first) & (lane < first + leaf)).astype(F32).astype(BF16)
                    pieces.append(part[:, begin : begin + LANES] * keep)
                else:
                    pieces.append(zero)
            rows.append(jnp.concatenate(pieces, axis=1))
        out.append(jnp.concatenate(rows, axis=0))
    return out


def pick(groups):
    shape = (FEATS, FEATS)
    feature = iota(shape, 0)
    want = jnp.full(shape, -1, jnp.int32)
    for g, row in enumerate(groups):
        want = jnp.where(feature // 3 == g, row + feature % 3, want)
    return (iota(shape, 1) == want).astype(F32).astype(BF16)


def features(position):
    row = iota(position.shape, 0)
    centred = jnp.where(row < 3, position - 0.5, 0.0)
    norm = -SCALE * jnp.sum(centred * centred, axis=0, keepdims=True)
    tail = jnp.where((row >= 3) & (row < 6), 1.0, 0.0)
    for r, part in enumerate(split3(norm)):
        tail = jnp.where(row == r, part, tail)
    own = jnp.concatenate([*split3(centred), tail], axis=0).astype(BF16)
    other = jnp.concatenate([*split3(centred * (2.0 * SCALE)), tail], axis=0).astype(BF16)
    source = dot(pick((0, 0, 0, 8, 8, 16, 24, 27)), own)
    target = dot(pick((0, 8, 16, 0, 8, 0, 27, 24)), other)
    return source, target


def set_features(position, src, tgt, begin):
    n = position.shape[1]
    for at in range(0, n, 512):
        end = min(at + 512, n)
        source, target = features(position[:, at:end])
        if tgt is not None:
            tgt[:, begin + at : begin + end] = target.astype(BF16)
        if src is not None:
            for lane in range(0, end - at, LANES):
                to = begin + at + lane
                src[to : to + LANES, :] = jnp.transpose(source[:, lane : lane + LANES]).astype(
                    BF16
                )


def pad_rows(points):
    return jnp.concatenate([points, jnp.zeros((8 - points.shape[0], points.shape[1]), F32)], axis=0)


def fill_block(src, tgt, row, lane, n_rows, mask, size, high, low, at):
    kernel = jnp.exp2(dot(src[pl.ds(row, n_rows), :], tgt[:, pl.ds(lane, LANES)]))
    if mask is not None:
        kernel = jnp.concatenate(
            [kernel[size * s : size * (s + 1)] * mask[s : s + 1] for s in range(n_rows // size)],
            axis=0,
        )
    high[pl.ds(at, n_rows), :], low[pl.ds(at, n_rows), :] = split2(kernel)


def in_turn(count, fill, use):
    half = count // 2
    for i in range(half):
        fill(i)
    for i in range(max(half, count - half)):
        if half + i < count:
            fill(half + i)
        if i < half:
            use(i)
    for i in range(half, count):
        use(i)


def use_block(coef, row, n_rows, high, low, at):
    return dot2(coef[:, pl.ds(row, n_rows)], high[pl.ds(at, n_rows), :], low[pl.ds(at, n_rows), :])


def upward_kernel(
    device, rhs_hbm, points_hbm, basis_hbm, transfer_hbm, prox_hbm, near_hbm, couple_hbm, roots_hbm,
    c3, c2, c1, tile0, first, second, table_high, table_low, big_high, big_low,
    rhs, points, near, couple, roots,
    basis, transfer, prox, padded, moved, sems, *, leaf, rank, starts,
):
    vectors = rhs.shape[0]
    coords = points.shape[0]
    span = FAN * leaf
    group = FAN * rank
    outs = {1: c1, 2: c2, 3: c3}
    copies = [
        pltpu.make_async_copy(source, to, sems.at[i])
        for i, (source, to) in enumerate(
            (
                (prox_hbm, prox),
                (transfer_hbm, transfer),
                (basis_hbm, basis),
                (rhs_hbm, rhs),
                (points_hbm, points),
                (near_hbm, near),
                (couple_hbm, couple),
                (roots_hbm, roots),
            )
        )
    ]
    for copy in copies:
        copy.start()
    padded[...] = jnp.zeros(padded.shape, F32)

    copies[0].wait()
    row = iota((8, LANES), 0)
    block = iota((8, LANES), 1) // rank
    shift = FAN - 1
    padded[: prox.shape[0], shift : shift + prox.shape[1]] = prox[...]
    flipped = jnp.transpose(padded[:LANES, :])
    for t in range(0, shift + prox.shape[1], 8):
        tile = flipped[t : t + 8]
        turns = [tile] + [pltpu.roll(tile, rank * s, 1) for s in range(1, FAN)]
        sums = []
        for c in range(coords):
            value = jnp.zeros((8, LANES), F32)
            for j in range(FAN):
                value = jnp.where((row % FAN == j) & (block == j), turns[(j - c) % FAN], value)
            value = value + pltpu.roll(value, 7, 0)
            sums.append(value + pltpu.roll(value, 6, 0))
        for half in range(8 // FAN):
            g = t // FAN + half
            place = jnp.zeros((8, LANES), F32)
            for c in range(coords):
                turn = (c - half * FAN) % 8
                value = pltpu.roll(sums[c], turn, 0) if turn else sums[c]
                place = jnp.where(row == c, value, place)
            if g == 0:
                root_place = place
            elif g < 2:
                c1[vectors:, :] = place
            elif g < 2 + FAN:
                c2[vectors:, (g - 2) * group : (g - 1) * group] = place
            else:
                at = (g - 2 - FAN) * group
                c3[vectors:, at : at + group] = place
    padded[:LANES, :] = jnp.zeros((LANES, LANES), F32)

    for copy in copies[1:]:
        copy.wait()
    for g in range(rhs.shape[1] // span):
        rows = slice(2 * g * group, (2 * g + 1) * group)
        high, low = block_rows(basis, g * span, leaf)
        big_high[rows, :] = high
        big_low[rows, :] = low
        c3[:vectors, g * group : (g + 1) * group] = dot2(
            stack2(rhs[:, g * span : (g + 1) * span]), high, low, NT
        )
    n_clusters = transfer.shape[1]
    padded[:, :n_clusters] = transfer[...]
    for a in range(0, rank, FAN):
        flipped = jnp.transpose(padded[a * rank : (a + FAN) * rank, :])
        for t in range(0, n_clusters, 8):
            tile = flipped[t : t + 8]
            turns = [tile] + [pltpu.roll(tile, rank * s, 1) for s in range(1, FAN)]
            low = (t // FAN - 1) % FAN
            up = (t // FAN) % FAN
            in_low = (row < FAN) & (block == low)
            in_up = (row >= FAN) & (block == up)
            for j in range(FAN):
                value = jnp.where(in_up, turns[(up - j) % FAN], 0.0)
                value = jnp.where(in_low, turns[(low - j) % FAN], value)
                moved[t : t + 8, a + j, :] = value
    for t in range(0, n_clusters, FAN):
        rows = slice(t * rank, t * rank + group)
        table_high[rows, :], table_low[rows, :] = split2(
            moved[t : t + FAN].reshape(group, LANES)
        )

    for level in range(LEVELS, 0, -1):
        source = outs[level]
        count = FAN ** (level - 1)
        base = (starts[level] - 1) * rank
        per = min(FAN, count)
        width = per * group
        for h in range(count // per):
            begin = h * width
            rows = slice(base + begin, base + begin + width)
            merged = dot2(
                stack2(source[:vectors, begin : begin + width]),
                table_high[rows, :],
                table_low[rows, :],
            )
            if level > 1:
                outs[level - 1][:vectors, h * group : (h + 1) * group] = merged
            else:
                root = merged

    last = (FAN - 1) * rank
    tile = jnp.where(block == 0, pltpu.roll(root[:8], LANES - last, 1), 0.0)
    tile = jnp.where(block == 1, pltpu.roll(root[8:16], LANES - last + rank, 1), tile)
    tile = jnp.where(block == 2, pltpu.roll(root_place, (FAN - 1) * rank, 1), tile)
    tile0[...] = tile

    rim = 2 * group
    halo = REACH * leaf

    def fill(send, tail):
        at = 0
        for ref, width in ((c3, rim), (c2, rim)):
            begin = ref.shape[1] - width if tail else 0
            send[:, at : at + width] = ref[:, begin : begin + width]
            at += width
        begin = points.shape[1] - halo if tail else 0
        send[:vectors, at : at + halo] = rhs[:, begin : begin + halo]
        send[vectors:, at : at + halo] = pad_rows(points[:, begin : begin + halo])

    @pl.when(device[0] % 2 == 0)
    def _():
        fill(first, True)
        fill(second, False)

    @pl.when(device[0] % 2 == 1)
    def _():
        fill(first, False)
        fill(second, True)

    at = 2 * rim + halo
    first[:, at : at + group] = c1[...]
    second[:, at : at + group] = c1[...]
    first[:8, at + group :] = tile
    first[8:, at + group :] = jnp.zeros((ROWS - 8, LANES), F32)


def middle_kernel(first, second, tile0, send, pair):
    width = second.shape[1]
    send[:, :width] = second[...]
    send[:, width:] = first[:, width - LANES : width]
    pair[0] = tile0[...]
    pair[1] = first[:8, width:]


def join_kernel(lower, upper, out):
    count = lower.shape[0]
    out[:count] = lower[...]
    out[count:] = upper[...]


def near_kernel(rhs, points, near, out, src, tgt, coef, mask, high, low, *, leaf, begin):
    halo = REACH * leaf
    width = coef.shape[1]
    count = width // halo - 2
    lanes = slice(begin * halo, begin * halo + width)
    set_features(pad_rows(points[:, lanes]), src, tgt, 0)
    coef[...] = stack2(rhs[:, lanes])
    for at in range(0, width, 512):
        end = min(at + 512, width)
        mask[:, at:end] = near_mask(near, begin * halo + at, end - at, leaf)

    def fill(g):
        row = g * halo
        target = row + halo
        fill_block(
            src, tgt, row, target, 3 * halo, mask[:, pl.ds(target, halo)], leaf,
            high, low, g * 3 * halo,
        )

    def use(g):
        row = g * halo
        out[:, pl.ds(row, halo)] = use_block(coef, row, 3 * halo, high, low, g * 3 * halo)

    in_turn(count, fill, use)


def near_mask(near, begin, width, leaf):
    rows = listed_mask(near, begin // leaf, width, leaf)
    slots = rows.shape[0]
    odd = (iota((8, width), 1) // leaf) % 2 == 1
    even_rows = jnp.concatenate([rows, jnp.zeros((8 - slots, width), F32)], axis=0)
    return jnp.where(odd, pltpu.roll(even_rows, 1, 0), even_rows)


def far_kernel(
    device, c3, couple, roots, out, usable,
    src, tgt, coef, mask, high, low, *, rank, base, xor, steps,
):
    group = FAN * rank
    vectors = out.shape[0]
    width = c3.shape[1]
    set_features(c3[vectors:, :], src, tgt, 0)
    coef[...] = stack2(c3[:vectors, :])
    slots = couple.shape[0]
    for at in range(0, width, 512):
        mask[:slots, at : at + 512] = listed_mask(couple, base + at // rank, 512, rank)

    def fill(q):
        begin = q * group
        target = begin + 2 * group
        fill_block(
            src, tgt, begin, target, 5 * group, mask[:, pl.ds(target, group)], rank,
            high, low, q * 5 * group,
        )

    def use(q):
        begin = q * group
        out[:, pl.ds(begin + 2 * group, group)] = use_block(
            coef, begin, 5 * group, high, low, q * 5 * group
        )

    count = width // group - 4
    in_turn(count, fill, use)
    n_roots = roots.shape[1]
    listed = (jnp.broadcast_to(roots[...], (8, n_roots)) >= 0).astype(F32).astype(BF16)
    for at in range(0, n_roots * rank, 512):
        shape = (n_roots, 512)
        source = at // rank + iota(shape, 1) // rank
        if xor:
            away = sum(((source >> i) & 1) * step for i, step in enumerate(steps))
            source = jnp.bitwise_xor(away, device[0])
        usable[:, at : at + 512] = dot(listed, (iota(shape, 0) == source).astype(F32).astype(BF16))


def edge_kernel(
    device, first, second, third, c3, c2, c1, rhs, points, near, couple,
    near_edge, g3_edge, g2, g1, ext, src, tgt, coef, high, low,
    *, leaf, rank, starts,
):
    group = FAN * rank
    rim = 2 * group
    halo = REACH * leaf
    vectors = rhs.shape[0]
    n3 = c3.shape[1]
    n2 = c2.shape[1]
    n_points = rhs.shape[1]
    l3 = 0
    r3 = l3 + 3 * rim
    l2 = r3 + 3 * rim
    ln = l2 + n2 + 2 * rim
    rn = ln + 3 * halo
    one = rn + 3 * halo
    here = 2 * rim + halo
    own = first[:, here : here + group]
    near_by = second[:, here : here + group]
    beyond = second[:, here + group : here + 2 * group]

    def rims(left, right, parts):
        for i, part in enumerate(parts):
            ext[:, one + i * group : one + (i + 1) * group] = part
        ext[:, l3 : l3 + rim] = left[:, :rim]
        ext[:, r3 + 2 * rim : r3 + 3 * rim] = right[:, :rim]
        ext[:, l2 : l2 + rim] = left[:, rim : 2 * rim]
        ext[:, l2 + rim + n2 : l2 + 2 * rim + n2] = right[:, rim : 2 * rim]
        ext[:, ln : ln + halo] = left[:, 2 * rim : 2 * rim + halo]
        ext[:, rn + 2 * halo : rn + 3 * halo] = right[:, 2 * rim : 2 * rim + halo]

    @pl.when(device[0] % 2 == 0)
    def _():
        rims(second, first, (beyond, near_by, c1[...], own, third[...]))

    @pl.when(device[0] % 2 == 1)
    def _():
        rims(first, second, (third[...], own, c1[...], near_by, beyond))

    ext[:, l3 + rim : l3 + 3 * rim] = c3[:, : 2 * rim]
    ext[:, r3 : r3 + 2 * rim] = c3[:, n3 - 2 * rim :]
    ext[:, l2 + rim : l2 + rim + n2] = c2[...]
    for to, begin in ((ln + halo, 0), (rn, n_points - 2 * halo)):
        ext[:vectors, to : to + 2 * halo] = rhs[:, begin : begin + 2 * halo]
        ext[vectors:, to : to + 2 * halo] = pad_rows(points[:, begin : begin + 2 * halo])
    set_features(ext[vectors:, :], src, tgt, 0)
    coef[...] = stack2(ext[:vectors, :])
    base3 = starts[3] - 1
    base2 = starts[2] - 1
    n_leaves = n_points // leaf
    jobs = []
    for i in range(2):
        for to, begin, cluster in ((i, l3, i * FAN), (2 + i, r3, (n3 // group - 2 + i) * FAN)):
            jobs.append((g3_edge, to * group, begin + i * group, 5 * group, rim, base3 + cluster))
    for q in range(n2 // group):
        jobs.append((g2, q * group, l2 + q * group, 5 * group, rim, base2 + q * FAN))
    jobs.append((g1, 0, one, 5 * group, rim, starts[1] - 1))
    jobs.append((near_edge, 0, ln, 3 * halo, halo, 0))
    jobs.append((near_edge, halo, rn, 3 * halo, halo, n_leaves - 2))
    at = 0
    for out, to, begin, n_rows, ahead, cluster in jobs:
        if out is near_edge:
            mask, size = near_mask(near, cluster * leaf, halo, leaf), leaf
        else:
            mask, size = listed_mask(couple, cluster, group, rank), rank
        fill_block(src, tgt, begin, begin + ahead, n_rows, mask, size, high, low, at)
        at += n_rows
    at = 0
    for out, to, begin, n_rows, ahead, cluster in jobs:
        out[:, to : to + LANES] = use_block(coef, begin, n_rows, high, low, at)
        at += n_rows


def root_parts(position, scale):
    row = iota(position.shape, 0)
    centred = jnp.where(row < 3, position - 0.5, 0.0)
    norm = split3(-SCALE * jnp.sum(centred * centred, axis=0, keepdims=True))
    return split3(centred * scale), norm, row


def root_target(position, rank):
    (high, mid, low), norm, row = root_parts(position, 2.0 * SCALE)
    tail = jnp.where(row < 3, 1.0, 0.0)
    for r, part in enumerate(norm):
        tail = jnp.where(row == 3 + r, part, tail)
    zero = jnp.zeros_like(high)
    columns = (high, high, high, tail, mid, mid, zero, zero, low, zero, zero, zero)
    return jnp.transpose(jnp.concatenate(columns, axis=0))[:rank].astype(BF16)


def couple_roots(tiles, usable, begin, target, ext, rank):
    n = tiles.shape[0] * rank
    block = iota((8, LANES), 1) // rank
    for at in range(0, tiles.shape[0], FAN):
        parts = [jnp.zeros((8, LANES), F32)] * 3
        for j in range(FAN):
            value = tiles[at + j]
            for i in range(3):
                turn = ((j - i) % FAN) * rank
                turned = pltpu.roll(value, turn, 1) if turn else value
                parts[i] = jnp.where(block == j, turned, parts[i])
        lanes = slice(at * rank, at * rank + LANES)
        for i in range(3):
            ext[8 * i : 8 * i + 8, lanes] = parts[i]
    total = None
    step = min(n, 512)
    for at in range(0, n, step):
        lanes = slice(at, at + step)
        (high, mid, low), norm, row = root_parts(ext[16:24, lanes], 1.0)
        tail = jnp.where((row >= 3) & (row < 6), 1.0, 0.0)
        for r, part in enumerate(norm):
            tail = jnp.where(row == r, part, tail)
        source = jnp.concatenate([high, mid, low, tail], axis=0).astype(BF16)
        kernel = jnp.exp2(dot(target[...], jnp.concatenate([source] * 3, axis=0)))
        both = stack2(ext[:16, lanes] * usable[0:1, begin + at : begin + at + step])
        share = dot2(both, *split2(kernel), NT)
        total = share if total is None else total + share
    return total


def way_kernel(table_high, table_low, _high, _low, way_high, way_low, *, rank, starts):
    group = FAN * rank

    shape = (rank, LANES)
    unit = (iota(shape, 1) % rank == iota(shape, 0)).astype(F32).astype(BF16)

    def turned(level, begin, count):
        at = (starts[level] - 1 + begin) * rank
        rows = slice(at, at + count * rank)
        parts = [dot(unit, table[rows, :], NT).astype(BF16) for table in (table_high, table_low)]
        return jnp.concatenate(parts, axis=0)

    count = FAN * FAN
    every = turned(3, 0, FAN * count)
    stages = (
        [every[:, q * group : (q + 1) * group] for q in range(count)],
        [turned(2, q, 1) for q in range(count)],
        [part for part in (turned(1, h, 1) for h in range(FAN)) for _ in range(FAN)],
    )
    at = 0
    n_rows = group
    for stage in stages:
        done = [
            split2(
                dot2(
                    stage[q],
                    way_high[2 * q * group + at : 2 * q * group + at + n_rows, :],
                    way_low[2 * q * group + at : 2 * q * group + at + n_rows, :],
                )
            )
            for q in range(count)
        ]
        at += n_rows
        n_rows = rank
        for q, (high, low) in enumerate(done):
            rows = slice(2 * q * group + at, 2 * q * group + at + rank)
            way_high[rows, :] = high
            way_low[rows, :] = low
    at += rank
    zero = jnp.zeros((rank, way_high.shape[1]), BF16)
    for q in range(count):
        rows = slice(2 * q * group + at, 2 * q * group + at + rank)
        way_high[rows, :] = zero
        way_low[rows, :] = zero


def down_kernel(
    tiles, usable, tile0, near_low, near_high, near_edge, g3, g3_edge, g2, g1, way_high, way_low,
    base, part, target, ext, *, leaf, rank,
):
    group = FAN * rank
    vectors = base.shape[0]
    target[...] = root_target(pltpu.roll(tile0[...], (FAN - 2) * rank, 1), rank)
    part[...] = couple_roots(tiles, usable, 0, target, ext, rank)
    count = FAN * FAN
    span = FAN * leaf
    halo = REACH * leaf
    block = iota((vectors, LANES), 1) // rank
    for q in range(count):
        if q < 2:
            own = g3_edge[:, q * group : (q + 1) * group]
        elif q >= count - 2:
            to = (q - count + 4) * group
            own = g3_edge[:, to : to + group]
        else:
            own = g3[:, q * group : (q + 1) * group]
        parent, child = q // FAN, q % FAN
        above = g2[:, parent * group : (parent + 1) * group]
        if child:
            above = pltpu.roll(above, (FAN - child) * rank, 1)
        top = g1[...]
        if parent != 1:
            top = pltpu.roll(top, (FAN + 1 - parent) % FAN * rank, 1)
        above = jnp.where(block == 0, above, jnp.where(block == 1, top, 0.0))
        rows = slice(2 * q * group, 2 * (q + 1) * group)
        lanes = slice(q * span, (q + 1) * span)
        base[:, lanes] = dot2(
            stack2(jnp.concatenate([own, above], axis=1)), way_high[rows, :], way_low[rows, :]
        )
    n_low = near_low.shape[1]
    n_high = near_high.shape[1]
    base[:, :halo] += near_edge[:, :halo]
    base[:, halo : halo + n_low] += near_low[...]
    base[:, halo + n_low : halo + n_low + n_high] += near_high[...]
    base[:, halo + n_low + n_high :] += near_edge[:, halo:]


def final_kernel(
    tiles, usable, part, target, base, way_high, way_low, out_hbm,
    ext, out, sems, *, rank,
):
    begin = tiles.shape[0] * rank
    both = stack2(part[...] + couple_roots(tiles, usable, begin, target, ext, rank))
    n = out.shape[1]
    span = way_high.shape[1]
    groups = n // span
    group = FAN * rank
    per = groups // sems.shape[0]
    copies = []
    for i in range(sems.shape[0]):
        for q in range(i * per, (i + 1) * per):
            at = 2 * q * group + group + 2 * rank
            rows = slice(at, at + rank)
            lanes = slice(q * span, (q + 1) * span)
            out[:, lanes] = base[:, lanes] + dot2(both, way_high[rows, :], way_low[rows, :])
        lanes = slice(i * per * span, (i + 1) * per * span)
        copies.append(pltpu.make_async_copy(out.at[:, lanes], out_hbm.at[:, lanes], sems.at[i]))
        copies[-1].start()
    for copy in copies:
        copy.wait()


def body(points, rhs, leaf_basis, transfer, proxies, near_list, couple_list, root_list):
    count = lax.axis_size("leaf")
    device = lax.axis_index("leaf").astype(jnp.int32)[None]
    rank = leaf_basis.shape[0]
    vectors, n_points = rhs.shape
    n_leaves = near_list.shape[0]
    leaf = n_points // n_leaves
    group = FAN * rank
    rim = 2 * group
    halo = REACH * leaf
    starts = [(FAN**level - 1) // (FAN - 1) for level in range(LEVELS + 1)]
    n_clusters = transfer.shape[2]
    n3 = FAN**3 * rank
    n2 = FAN**2 * rank
    flat_transfer = transfer.reshape(rank * rank, n_clusters)
    flat_prox = proxies.reshape(proxies.shape[0] * rank, proxies.shape[2])

    vmem = pl.BlockSpec(memory_space=pltpu.VMEM)
    smem = pl.BlockSpec(memory_space=pltpu.SMEM)

    def shape(*dims, dtype=F32):
        return jax.ShapeDtypeStruct(dims, dtype)

    def call(kernel, n_in, outs, scratch, mib, scalar=True, space=vmem, to=vmem):
        return pl.pallas_call(
            kernel,
            out_shape=outs,
            in_specs=([smem] if scalar else []) + [space] * n_in,
            out_specs=jax.tree.map(lambda _: to, outs),
            scratch_shapes=scratch,
            compiler_params=pltpu.CompilerParams(vmem_limit_bytes=mib << 20),
        )

    padded_clusters = -(-n_clusters // 8) * 8
    width = 2 * rim + halo + group
    span = FAN * leaf
    n_big = n_points // span * 2 * group
    inputs = (
        rhs, points, leaf_basis, flat_transfer, flat_prox, near_list.T, couple_list.T, root_list
    )
    (
        c3, c2, c1, tile0, to_first, to_second, table_high, table_low, big_high, big_low,
        rhs_v, points_v, near_v, couple_v, roots_v,
    ) = call(
        lambda *refs: upward_kernel(*refs, leaf=leaf, rank=rank, starts=starts),
        8,
        (
            shape(ROWS, n3),
            shape(ROWS, n2),
            shape(ROWS, group),
            shape(8, LANES),
            shape(ROWS, width + LANES),
            shape(ROWS, width),
            shape(n_clusters * rank, LANES, dtype=BF16),
            shape(n_clusters * rank, LANES, dtype=BF16),
            shape(n_big, span, dtype=BF16),
            shape(n_big, span, dtype=BF16),
            *(shape(*inputs[i].shape, dtype=inputs[i].dtype) for i in (0, 1, 5, 6, 7)),
        ),
        [
            *(pltpu.VMEM(inputs[i].shape, F32) for i in (2, 3, 4)),
            pltpu.VMEM((rank * rank, LANES), F32),
            pltpu.VMEM((padded_clusters, rank, LANES), F32),
            pltpu.SemaphoreType.DMA((8,)),
        ],
        16,
        space=pl.BlockSpec(memory_space=pltpu.HBM),
    )(device, *(pltpu.with_memory_space_constraint(array, pltpu.HBM) for array in inputs))

    def swap(value, step):
        return lax.ppermute(value, "leaf", [(i, i ^ step) for i in range(count)])

    first = swap(to_first, 1)
    send, gathered = call(
        middle_kernel, 3, (shape(ROWS, width + group), shape(2, 8, LANES)), [], 2, scalar=False
    )(first, to_second, tile0)
    xor = count & (count - 1) == 0

    def join(lower, upper):
        return call(
            join_kernel, 2, shape(2 * lower.shape[0], 8, LANES), [], 2, scalar=False
        )(lower, upper)

    pairs = [(i, i + 1) for i in range(1, count - 1, 2)]
    second = lax.ppermute(send, "leaf", pairs + [(j, i) for i, j in pairs])
    third = swap(second[:, width - group : width], 1)
    steps = [1 << i for i in range(count.bit_length() - 1)]
    if len(steps) > 3:
        steps[1], steps[2] = steps[2], steps[1]
    if xor:
        for i, step in enumerate(steps[1:], 1):
            last = i == len(steps) - 1
            other = swap(gathered, step)
            if not last:
                gathered = join(gathered, other)
    else:
        everything = lax.all_gather(tile0, "leaf", axis=0)
        gathered, other = everything[: count // 2], everything[count // 2 :]

    n_groups = n_points // halo

    def near_part(begin, n_near):
        lanes = (n_near + 2) * halo
        return call(
            lambda *refs: near_kernel(
                *refs, leaf=leaf, begin=begin
            ),
            3,
            shape(vectors, n_near * halo),
            [
                pltpu.VMEM((lanes, FEATS), BF16),
                pltpu.VMEM((FEATS, lanes), BF16),
                pltpu.VMEM((2 * vectors, lanes), BF16),
                pltpu.VMEM((8, lanes), F32),
                pltpu.VMEM((n_near * 3 * halo, LANES), BF16),
                pltpu.VMEM((n_near * 3 * halo, LANES), BF16),
            ],
            12,
            scalar=False,
        )(rhs_v, points_v, near_v)

    half = (n_groups - 2) // 2
    near_low = near_part(0, half)
    near_high = near_part(half, n_groups - 2 - half)

    n_all = count * rank
    n_far = FAN**2 - 4
    g3, usable = call(
        lambda *refs: far_kernel(
            *refs, rank=rank, base=starts[3] - 1, xor=xor, steps=steps
        ),
        3,
        (
            shape(vectors, n3),
            shape(8, n_all),
        ),
        [
            pltpu.VMEM((n3, FEATS), BF16),
            pltpu.VMEM((FEATS, n3), BF16),
            pltpu.VMEM((2 * vectors, n3), BF16),
            pltpu.VMEM((ROWS, n3), F32),
            pltpu.VMEM((n_far * 5 * group, LANES), BF16),
            pltpu.VMEM((n_far * 5 * group, LANES), BF16),
        ],
        12,
    )(device, c3, couple_v, roots_v)

    n_ext = 6 * rim + n2 + 2 * rim + 6 * halo + 5 * group
    n_rows = (5 + n2 // group) * 5 * group + 2 * 3 * halo
    near_edge, g3_edge, g2, g1 = call(
        lambda *refs: edge_kernel(*refs, leaf=leaf, rank=rank, starts=starts),
        10,
        (
            shape(vectors, 2 * halo),
            shape(vectors, 2 * rim),
            shape(vectors, n2),
            shape(vectors, group),
        ),
        [
            pltpu.VMEM((ROWS, n_ext), F32),
            pltpu.VMEM((n_ext, FEATS), BF16),
            pltpu.VMEM((FEATS, n_ext), BF16),
            pltpu.VMEM((2 * vectors, n_ext), BF16),
            pltpu.VMEM((n_rows, LANES), BF16),
            pltpu.VMEM((n_rows, LANES), BF16),
        ],
        12,
    )(
        device, first, second, third, c3, c2, c1, rhs_v, points_v, near_v, couple_v,
    )

    n_half = count // 2 * rank
    scratch = [pltpu.VMEM((ROWS, n_half), F32)]
    way_high, way_low = pl.pallas_call(
        lambda *refs: way_kernel(*refs, rank=rank, starts=starts),
        out_shape=(shape(n_big, span, dtype=BF16), shape(n_big, span, dtype=BF16)),
        in_specs=[vmem] * 4,
        out_specs=(vmem, vmem),
        input_output_aliases={2: 0, 3: 1},
        compiler_params=pltpu.CompilerParams(vmem_limit_bytes=12 << 20),
        name="way",
    )(table_high, table_low, big_high, big_low)
    base, part, target = call(
        lambda *refs: down_kernel(*refs, leaf=leaf, rank=rank),
        12,
        (
            shape(vectors, n_points),
            shape(vectors, rank),
            shape(rank, 3 * FEATS, dtype=BF16),
        ),
        scratch,
        12,
        scalar=False,
    )(
        gathered, usable, tile0, near_low, near_high, near_edge, g3, g3_edge, g2, g1,
        way_high, way_low,
    )
    return call(
        lambda *refs: final_kernel(*refs, rank=rank),
        7,
        shape(vectors, n_points),
        [*scratch, pltpu.VMEM((vectors, n_points), F32), pltpu.SemaphoreType.DMA((4,))],
        12,
        scalar=False,
        to=pl.BlockSpec(memory_space=pltpu.HBM),
    )(other, usable, part, target, base, way_high, way_low)


def solution(mesh):
    in_specs = (
        P(None, "leaf"),
        P(None, "leaf"),
        P(None, "leaf"),
        P(None, None, "leaf"),
        P(None, None, "leaf"),
        P("leaf", None),
        P("leaf", None),
        P("leaf", None),
    )
    out_specs = P(None, "leaf")
    return jax.shard_map(body, mesh=mesh, in_specs=in_specs, out_specs=out_specs, check_vma=False)
```
